128 devices in a mesh: wide: 8 (over z_lo, x), narrow: 16 (over y, z_hi, core).
Axes of the slice: x: 4, y: 4, z: 4 (z_hi: 2, z_lo: 2; z = z_hi * 2 + z_lo), core: 2. Of those that a mesh axis runs over, the one named last changes fastest.
Arguments:
- seafloor_ops: bfloat16 [512, 4, 2, 128, 2048], P(None, None, None, 'wide', 'narrow'), may hold values from -0.25 to 0.25
- sensor_data: bfloat16 [512, 4, 2, 256], P('wide', None, None, 'narrow'), may hold values from -6 to 6
- column_freq: int32 [256], replicated, may hold values from 0 to 3
- row_owner: int32 [512], replicated, may hold values from 0 to 511, each once
- coef_class: int32 [128, 2048], P('wide', 'narrow'), may hold values from 0 to 7
- coef_table: float32 [8], replicated, may hold values from 0.02 to 0.24
Outputs:
- hessian_cols: bfloat16 [512, 4, 2, 256], P('wide', None, None, 'narrow')
- prior_field: bfloat16 [256, 128, 2048], P(None, 'wide', 'narrow')
The draws below stay inside these ranges and needn't reach their ends.
All inputs are finite; a program needn't handle non-finite values.
Results may differ from the reference program's by a relative error of at most 0.0026.
Values may be sent and summed in bfloat16 or wider, within the bound.
No kernel may reach another device: no remote copies, remote signals or barrier semaphores. Data moves between devices by JAX's collectives and lax.ppermute only.
A program may use at most 128 MiB of HBM per device.

```python
import math
import jax
import jax.numpy as jnp

SENS = 512
FREQ = 4
COLS = 256
NCLASS = 8
SWEEPS = 3
NX = 128
NY = 2048


def touch_ends(entries, key, least, top_value):
    place = [jax.random.randint(jax.random.fold_in(key, axis), (), 0, length) for axis, length in enumerate(entries.shape)]
    longest = entries.shape.index(max(entries.shape))
    neighbour = place[:longest] + [(place[longest] + 1) % entries.shape[longest]] + place[longest + 1:]
    return entries.at[tuple(place)].set(least).at[tuple(neighbour)].set(top_value)


def spiked(entries, own_key, source, target, shards_of, factor):
    owner, partner = [(jnp.arange(entries.shape[axis_at]) // (entries.shape[axis_at] // shards_of)).reshape([-1 if axis == axis_at else 1 for axis in range(entries.ndim)]) for axis_at in (source, target)]
    chosen = jax.random.permutation(own_key, shards_of)[partner]
    strong = (owner == chosen) | (owner == (partner + shards_of // 2) % shards_of)
    return jnp.where(strong, factor * entries, entries)


def steps_of(stream_key, dims, split, low, high):
    def one(dim, shards_of):
        draws = jax.random.uniform(jax.random.fold_in(jax.random.fold_in(stream_key, 6), dim), (shards_of,), jnp.float32, low / len(split), high / len(split))
        return jnp.repeat(jnp.exp(draws), dims[dim] // shards_of).reshape((-1,) + (1,) * (len(dims) - dim - 1))

    gain = one(*split[0])
    for cut in split[1:]:
        gain = gain * one(*cut)
    return gain


def noise(rng, dims, spread, bound, cuts=(), held_as=jnp.bfloat16):
    drawn = spread * jax.random.normal(rng, dims, jnp.float32)
    if cuts:
        drawn = drawn * steps_of(rng, dims, cuts, -0.22, 0.18)
    return jnp.clip(drawn, -bound, bound).astype(held_as)


def noise_with(rng, shape, spread, reach, split, heavy, kind=jnp.bfloat16):
    array = spread * jax.random.normal(rng, shape, jnp.float32)
    if split:
        array = array * steps_of(rng, shape, split, -0.22, 0.18)
    return jnp.clip(spiked(array, jax.random.fold_in(rng, 3), *heavy), -reach, reach).astype(kind)


def setup_inputs(seed: int = 0) -> dict:
    seeds = jax.random.split(jax.random.key(seed), 7)
    return {
        "seafloor_ops": noise_with(seeds[0], (SENS, FREQ, 2, NX, NY), (2 * SENS) ** -0.5, 0.25, ((3, 8), (4, 16)), (3, 0, 8, 2.0)),
        "sensor_data": noise(seeds[1], (SENS, FREQ, 2, COLS), 1.0, 6.0, ((0, 8), (3, 16))),
        "column_freq": touch_ends(jax.random.randint(seeds[2], (COLS,), 0, FREQ), jax.random.fold_in(seeds[2], 1), 0, FREQ - 1).astype(jnp.int32),
        "row_owner": jax.random.permutation(seeds[3], SENS).astype(jnp.int32),
        "coef_class": touch_ends(jax.random.randint(seeds[4], (NX, NY), 0, NCLASS), jax.random.fold_in(seeds[4], 1), 0, NCLASS - 1).astype(jnp.int32),
        "coef_table": jnp.clip(jnp.exp(jax.random.uniform(seeds[5], (NCLASS,), jnp.float32, math.log(0.02), math.log(0.24))), 0.02, 0.24),
    }


def sweep(padded, coef):
    center = padded[:, 1:-1, 1:-1]
    inner = coef[1:-1, 1:-1]
    change = jnp.minimum(inner, coef[2:, 1:-1]) * (padded[:, 2:, 1:-1] - center)
    change = change + jnp.minimum(inner, coef[:-2, 1:-1]) * (padded[:, :-2, 1:-1] - center)
    change = change + jnp.minimum(inner, coef[1:-1, 2:]) * (padded[:, 1:-1, 2:] - center)
    change = change + jnp.minimum(inner, coef[1:-1, :-2]) * (padded[:, 1:-1, :-2] - center)
    return center + change


def lookup(coef_class, coef_table):
    classes = jnp.arange(NCLASS, dtype=jnp.int32)
    picks = (coef_class[None, :, :] == classes[:, None, None]).astype(jnp.float32)
    return jnp.sum(picks * coef_table[:, None, None], axis=0)


def reference(seafloor_ops, sensor_data, column_freq, row_owner, coef_class, coef_table):
    sensor_rows = jnp.take(sensor_data, row_owner, axis=0)
    freq_mask = (column_freq[None, :] == jnp.arange(FREQ, dtype=jnp.int32)[:, None]).astype(jnp.bfloat16)
    probes = sensor_rows * freq_mask[None, :, None, :]
    ops_flat = seafloor_ops.reshape(SENS * FREQ * 2, NX * NY)
    adjoint = jnp.dot(probes.reshape(SENS * FREQ * 2, COLS).T, ops_flat, preferred_element_type=jnp.float32)
    kappa = jnp.pad(lookup(coef_class, coef_table), 1)
    field = adjoint.reshape(COLS, NX, NY)
    for turn in range(SWEEPS):
        field = sweep(jnp.pad(field, ((0, 0), (1, 1), (1, 1))), kappa)
    prior_field = field.astype(jnp.bfloat16)
    quad_weight = 2.0 * SENS / (NX * NY)
    forward = jnp.dot(ops_flat, prior_field.reshape(COLS, NX * NY).T, preferred_element_type=jnp.float32) * quad_weight
    stored = jnp.zeros((SENS, FREQ, 2, COLS), jnp.float32).at[row_owner].set(forward.reshape(SENS, FREQ, 2, COLS))
    return stored.astype(jnp.bfloat16), prior_field
```

```python
import jax
import jax.numpy as jnp
from jax import lax
from jax.experimental import pallas as pl
from jax.experimental.pallas import tpu as pltpu
from jax.sharding import PartitionSpec as P

SWEEPS = 3
BOTH = ("wide", "narrow")
F32 = jnp.float32
BF16 = jnp.bfloat16
WHOLE = pl.BlockSpec(memory_space=pltpu.VMEM)
SCALARS = pl.BlockSpec(memory_space=pltpu.SMEM)
PX, PY = 16, 128
COLS, FREQ, NW, KW = 256, 4, 8, 512
STRIP = 24


def params(mib):
    return pltpu.CompilerParams(vmem_limit_bytes=mib << 20)


def relayout_body(inv, ops, out, buf, sems):
    group = pl.program_id(0)
    per = buf.shape[2]

    def fetch(which, slot):
        def one(j, _):
            sensor = inv[which * per + j]
            pltpu.make_async_copy(ops.at[sensor], buf.at[slot, :, j], sems.at[slot]).start()
            return 0

        lax.fori_loop(0, per, one, 0, unroll=8)

    @pl.when(group == 0)
    def _():
        fetch(0, 0)

    @pl.when(group + 1 < pl.num_programs(0))
    def _():
        fetch(group + 1, (group + 1) % 2)

    slot = group % 2
    pltpu.make_async_copy(buf.at[slot], buf.at[slot], sems.at[slot]).wait()
    for f in range(FREQ):
        block = buf[slot, f].reshape(per * 2, PX, PY)
        start = pl.multiple_of(group * KW + f * per * 2, per * 2)
        out[:, pl.ds(start, per * 2), :] = jnp.swapaxes(block, 0, 1)


def relayout(ops, inv):
    sens = ops.shape[0]
    per = sens // NW
    return pl.pallas_call(
        relayout_body,
        grid=(NW,),
        in_specs=[SCALARS, pl.BlockSpec(memory_space=pl.ANY)],
        out_specs=WHOLE,
        out_shape=jax.ShapeDtypeStruct((PX, sens * FREQ * 2, PY), BF16),
        scratch_shapes=[
            pltpu.VMEM((2, FREQ, per, 2, PX, PY), BF16),
            pltpu.SemaphoreType.DMA((2,)),
        ],
        compiler_params=params(30),
    )(inv, ops)


def strip_lane(rows):
    left = (rows >= 3) & (rows < 12)
    right = (rows >= 12) & (rows < 21)
    return jnp.where(left, rows - 3, jnp.where(right, rows + (PY - 21), -1))


def adjoint_body(gathered, freq, ops, classes, field, strips, y_up, y_down, probes):
    step = pl.program_id(0)

    @pl.when(step == 0)
    def _():
        for w in range(NW):
            for f in range(FREQ):
                at = w * KW + f * 128
                mine = freq[...] == f
                probes[:, at : at + 128] = jnp.where(mine, gathered[w], 0).astype(BF16)

    pair = jnp.concatenate([ops[2 * step], ops[2 * step + 1]], axis=1)
    both = jnp.dot(probes[...], pair, preferred_element_type=F32)
    rows = lax.broadcasted_iota(jnp.int32, (STRIP, PY), 0)
    lanes = lax.broadcasted_iota(jnp.int32, (STRIP, PY), 1)
    pick = (strip_lane(rows) == lanes).astype(F32)
    nt = (((1,), (1,)), ((), ()))
    for h in range(2):
        x = 2 * step + h
        mine = both[:, h * PY : (h + 1) * PY]
        field[x] = mine
        strip = lax.dot_general(pick, mine, nt, precision=lax.Precision.HIGHEST, preferred_element_type=F32)
        row = jnp.broadcast_to(classes[pl.ds(x, 1), :], (PY, PY))
        label = lax.dot_general(pick, row, nt, preferred_element_type=F32)
        parts = (strip[:, :128], strip[:, 128:], label)
        for t in range(3):
            strips[x, t] = parts[t]
        pad = jnp.zeros((7, 128), F32)
        y_up[x] = jnp.concatenate([p[18:21] for p in parts] + [pad], axis=0).astype(BF16)
        y_down[x] = jnp.concatenate([p[3:6] for p in parts] + [pad], axis=0).astype(BF16)


def adjoint(gathered, freq, ops, classes):
    edge = jax.ShapeDtypeStruct((PX, 16, 128), BF16)
    edge_spec = pl.BlockSpec((PX, 16, 128), lambda i: (0, 0, 0))
    return pl.pallas_call(
        adjoint_body,
        grid=(PX // 2,),
        in_specs=[WHOLE] * 4,
        out_specs=(WHOLE, WHOLE, edge_spec, edge_spec),
        out_shape=(
            jax.ShapeDtypeStruct((PX, COLS, PY), F32),
            jax.ShapeDtypeStruct((PX, 3, STRIP, 128), F32),
            edge,
            edge,
        ),
        scratch_shapes=[pltpu.VMEM((COLS, NW * KW), BF16)],
        compiler_params=params(30),
    )(gathered, freq, ops, classes)


XROWS = COLS + 16 + 3 * STRIP


def edges_body(field, strips, before, after, classes, whole_strips, x_up, x_down):
    for x in range(PX):
        for t in range(3):
            low = before[x].astype(F32)[3 * t : 3 * t + 3]
            high = after[x].astype(F32)[3 * t : 3 * t + 3]
            whole_strips[x, t] = jnp.concatenate([low, strips[x, t, 3:21, :], high], axis=0)
    for first, out in ((PX - 3, x_up), (0, x_down)):
        for j in range(3):
            x = first + j
            out[j, :COLS] = field[x].astype(BF16)
            out[j, COLS : COLS + 16] = jnp.broadcast_to(classes[x : x + 1, :], (16, PY)).astype(BF16)
            for t in range(3):
                at = COLS + 16 + t * STRIP
                out[j, at : at + STRIP] = whole_strips[x, t].astype(BF16)


def edges(field, strips, before, after, classes):
    send = jax.ShapeDtypeStruct((3, XROWS, 128), BF16)
    return pl.pallas_call(
        edges_body,
        in_specs=[WHOLE] * 5,
        out_specs=(WHOLE, pl.BlockSpec(), pl.BlockSpec()),
        out_shape=(jax.ShapeDtypeStruct((PX, 3, STRIP, 128), F32), send, send),
        compiler_params=params(30),
    )(field, strips, before, after, classes)


def table_of(labels, table):
    kappa = jnp.zeros(labels.shape, F32)
    for j in range(8):
        kappa = jnp.where(labels == float(j + 1), table[j], kappa)
    return kappa


def weights(here, up, down, left, right):
    four = [jnp.minimum(here, n) for n in (up, down, left, right)]
    return [1.0 - (four[0] + four[1] + four[2] + four[3])] + four


def smooth(value, load, axis, size):
    for turn in range(SWEEPS):
        fresh = []
        for i in range(1, len(value) - 1):
            m = load(i + turn)
            mid = value[i]
            left = pltpu.roll(mid, 1, axis)
            right = pltpu.roll(mid, size - 1, axis)
            a = m[0] * mid + m[1] * value[i - 1]
            b = m[2] * value[i + 1] + m[3] * left
            fresh.append(a + (b + m[4] * right))
        value = fresh
    return value


def sweep_body(table, field, strips, above, below, classes, prior, prior_out, main_w, strip_w):
    ext = PX + 6
    label = [above[j, COLS : COLS + 8].astype(F32) for j in range(3)]
    label += [jnp.broadcast_to(classes[x : x + 1, :], (8, PY)) for x in range(PX)]
    label += [below[j, COLS : COLS + 8].astype(F32) for j in range(3)]
    kappa = [table_of(v, table) for v in label]
    for i in range(1, ext - 1):
        k = kappa[i]
        ws = weights(k, kappa[i - 1], kappa[i + 1], pltpu.roll(k, 1, 1), pltpu.roll(k, PY - 1, 1))
        for d in range(5):
            main_w[i, d] = ws[d]
    at = COLS + 16

    def strip_rows(t):
        lo, hi = at + t * STRIP, at + (t + 1) * STRIP
        return (
            [above[j, lo:hi].astype(F32) for j in range(3)]
            + [strips[x, t] for x in range(PX)]
            + [below[j, lo:hi].astype(F32) for j in range(3)]
        )

    kappa = [table_of(v, table) for v in strip_rows(2)]
    for i in range(1, ext - 1):
        k = kappa[i]
        ws = weights(k, kappa[i - 1], kappa[i + 1], pltpu.roll(k, 1, 0), pltpu.roll(k, STRIP - 1, 0))
        for d in range(5):
            strip_w[i, d] = ws[d]
    edge = [smooth(strip_rows(t), lambda i: [strip_w[i, d] for d in range(5)], 0, STRIP) for t in range(2)]
    rows = lax.broadcasted_iota(jnp.int32, (STRIP, PY), 0)
    lanes = lax.broadcasted_iota(jnp.int32, (STRIP, PY), 1)
    pick = (strip_lane(rows) == lanes).astype(BF16)
    tn = (((0,), (0,)), ((), ()))
    for x in range(PX):
        both = jnp.concatenate([edge[0][x], edge[1][x]], axis=1).astype(BF16)
        prior[x] = lax.dot_general(both, pick, tn, preferred_element_type=F32).astype(BF16)

    def columns(g, _):
        c = pl.multiple_of(g * 16, 16)
        value = [above[j, pl.ds(c, 16), :].astype(F32) for j in range(3)]
        value += [field[x, pl.ds(c, 16), :] for x in range(PX)]
        value += [below[j, pl.ds(c, 16), :].astype(F32) for j in range(3)]

        def load(i):
            return [jnp.concatenate([main_w[i, d]] * 2, axis=0) for d in range(5)]

        value = smooth(value, load, 1, PY)
        lane = lax.broadcasted_iota(jnp.int32, (16, PY), 1)
        inner = (lane >= 3) & (lane < PY - 3)
        for x in range(PX):
            at_edge = prior[x, pl.ds(c, 16), :].astype(F32)
            prior[x, pl.ds(c, 16), :] = jnp.where(inner, value[x], at_edge).astype(BF16)
        return 0

    lax.fori_loop(0, COLS // 16, columns, 0)
    prior_out[...] = jnp.swapaxes(prior[...], 0, 1)


def sweeps(table, field, strips, above, below, classes):
    ext = PX + 6
    return pl.pallas_call(
        sweep_body,
        in_specs=[SCALARS] + [WHOLE] * 5,
        out_specs=(WHOLE, pl.BlockSpec()),
        out_shape=(
            jax.ShapeDtypeStruct((PX, COLS, PY), BF16),
            jax.ShapeDtypeStruct((COLS, PX, PY), BF16),
        ),
        scratch_shapes=[pltpu.VMEM((ext, 5, 8, PY), F32), pltpu.VMEM((ext, 5, STRIP, PY), F32)],
        compiler_params=params(30),
    )(table, field, strips, above, below, classes)


def forward_body(prior, ops, out):
    group = pl.program_id(0)
    rows = pl.ds(pl.multiple_of(group * KW, KW), KW)
    left = jnp.concatenate([prior[x] for x in range(PX)], axis=1)
    right = jnp.concatenate([ops[x, rows, :] for x in range(PX)], axis=1)
    nt = (((1,), (1,)), ((), ()))
    out[0] = lax.dot_general(left, right, nt, preferred_element_type=F32).astype(BF16)


def forward(prior, ops):
    return pl.pallas_call(
        forward_body,
        grid=(NW,),
        in_specs=[WHOLE, WHOLE],
        out_specs=pl.BlockSpec((1, COLS, KW), lambda i: (i, 0, 0)),
        out_shape=jax.ShapeDtypeStruct((NW, COLS, KW), BF16),
        compiler_params=params(30),
    )(prior, ops)


def shifted(value, axis, step):
    size = lax.axis_size(axis)
    return lax.ppermute(value, axis, [(i, i + step) for i in range(size) if 0 <= i + step < size])


def on_device(seafloor_ops, sensor_data, column_freq, row_owner, coef_class, coef_table):
    sens = seafloor_ops.shape[0]
    per, own = sensor_data.shape[0], sensor_data.shape[3]
    quad_weight = 2.0 * sens / (PX * lax.axis_size("wide") * PY * lax.axis_size("narrow"))
    my_freq = lax.dynamic_slice_in_dim(column_freq, lax.axis_index("narrow") * own, own)
    mask = my_freq[None, None, None, :] == jnp.arange(FREQ, dtype=jnp.int32)[None, :, None, None]
    chosen = jnp.sum(jnp.where(mask, sensor_data, 0).astype(F32), axis=1).astype(BF16)
    block = chosen.reshape(per * 2, own).T
    sent = jnp.broadcast_to(block[None], (128,) + block.shape)
    gathered = lax.all_to_all(sent, BOTH, 0, 0, tiled=True).reshape(NW, COLS, per * 2)

    ids = jnp.arange(sens, dtype=jnp.int32)
    inverse = jnp.sum(jnp.where(row_owner[None, :] == ids[:, None], ids[None, :], 0), axis=1)
    classes = (coef_class + 1).astype(F32)

    ops = relayout(seafloor_ops, inverse)
    field, strips, y_up, y_down = adjoint(gathered, column_freq.reshape(COLS, 1), ops, classes)
    before = shifted(y_up, "narrow", 1)
    after = shifted(y_down, "narrow", -1)
    strips, x_up, x_down = edges(field, strips, before, after, classes)
    above = shifted(x_up, "wide", 1)
    below = shifted(x_down, "wide", -1)
    prior, prior_field = sweeps(coef_table, field, strips, above, below, classes)
    partial_value = forward(prior, ops)
    pieces = lax.all_to_all(partial_value.reshape(128, own, KW), BOTH, 0, 0, tiled=True)
    total = jnp.sum(pieces.astype(F32), axis=0) * quad_weight
    hessian = total.astype(BF16).reshape(own, FREQ, per, 2).transpose(2, 1, 3, 0)
    return hessian, prior_field


def solution(mesh):
    placed = (
        P(None, None, None, "wide", "narrow"),
        P("wide", None, None, "narrow"),
        P(),
        P(),
        P("wide", "narrow"),
        P(),
    )
    return jax.shard_map(
        on_device,
        mesh=mesh,
        in_specs=placed,
        out_specs=(P("wide", None, None, "narrow"), P(None, "wide", "narrow")),
        check_vma=False,
    )
```

```python
import jax
import jax.numpy as jnp
from jax import lax
from jax.experimental import pallas as pl
from jax.experimental.pallas import tpu as pltpu
from jax.sharding import PartitionSpec as P

SWEEPS = 3
WIDE, NARROW = ("z_lo", "x"), ("y", "z_hi", "core")
BOTH = WIDE + NARROW
CHIPS = WIDE + NARROW[:2]
F32 = jnp.float32
BF16 = jnp.bfloat16
WHOLE = pl.BlockSpec(memory_space=pltpu.VMEM)
SCALARS = pl.BlockSpec(memory_space=pltpu.SMEM)
PX, PY = 16, 128
COLS, FREQ, NW, KW = 256, 4, 8, 512
STRIP = 24


def params(mib):
    return pltpu.CompilerParams(vmem_limit_bytes=mib << 20)


def strip_lane(rows):
    left = (rows >= 3) & (rows < 12)
    right = (rows >= 12) & (rows < 21)
    return jnp.where(left, rows - 3, jnp.where(right, rows + (PY - 21), -1))


def adjoint_body(inv, gathered, freq, stored, classes, ops, field, strips, y_up, y_down, buf, sems, probes):
    group = pl.program_id(0)
    per = buf.shape[2]

    def fetch(which, slot):
        def one(j, _):
            sensor = inv[which * per + j]
            pltpu.make_async_copy(stored.at[sensor], buf.at[slot, :, j], sems.at[slot]).start()
            return 0

        lax.fori_loop(0, per, one, 0, unroll=8)

    @pl.when(group == 0)
    def _():
        fetch(0, 0)
        field[...] = jnp.zeros_like(field)

    @pl.when(group + 1 < pl.num_programs(0))
    def _():
        fetch(group + 1, (group + 1) % 2)

    slot = group % 2
    block = gathered[group]
    for f in range(FREQ):
        probes[:, f * 128 : f * 128 + 128] = jnp.where(freq[...] == f, block, 0).astype(BF16)
    pltpu.make_async_copy(buf.at[slot], buf.at[slot], sems.at[slot]).wait()
    rows = pl.ds(pl.multiple_of(group * KW, KW), KW)
    for f in range(FREQ):
        start = pl.multiple_of(group * KW + f * per * 2, per * 2)
        tile = buf[slot, f].reshape(per * 2, PX, PY)
        ops[:, pl.ds(start, per * 2), :] = jnp.swapaxes(tile, 0, 1)
    for x in range(0, PX, 2):
        pair = jnp.concatenate([ops[x, rows, :], ops[x + 1, rows, :]], axis=1)
        both = jnp.dot(probes[...], pair, preferred_element_type=F32)
        field[x] += both[:, :PY]
        field[x + 1] += both[:, PY:]

    @pl.when(group == pl.num_programs(0) - 1)
    def _():
        line = lax.broadcasted_iota(jnp.int32, (STRIP, 2 * PY), 0)
        lanes = lax.broadcasted_iota(jnp.int32, (STRIP, 2 * PY), 1)
        pick = (strip_lane(line) == lanes % PY).astype(F32).astype(BF16)
        nt = (((1,), (1,)), ((), ()))
        for x in range(PX):
            mine = field[x]
            high = mine.astype(BF16)
            low = (mine - high.astype(F32)).astype(BF16)
            strip = lax.dot_general(pick, jnp.concatenate([high, low], axis=1), nt, preferred_element_type=F32)
            row = jnp.broadcast_to(classes[x : x + 1, :], (PY, PY)).astype(BF16)
            label = lax.dot_general(pick[:, :PY], row, nt, preferred_element_type=F32)
            parts = (strip[:, :128], strip[:, 128:], label)
            for t in range(3):
                strips[x, t] = parts[t]
            pad = jnp.zeros((7, 128), F32)
            y_up[x] = jnp.concatenate([p[18:21] for p in parts] + [pad], axis=0).astype(BF16)
            y_down[x] = jnp.concatenate([p[3:6] for p in parts] + [pad], axis=0).astype(BF16)


def adjoint(inv, gathered, freq, stored, classes):
    sens = stored.shape[0]
    per = sens // NW
    edge = jax.ShapeDtypeStruct((PX, 16, 128), BF16)
    edge_spec = pl.BlockSpec((PX, 16, 128), lambda i: (0, 0, 0))
    return pl.pallas_call(
        adjoint_body,
        grid=(NW,),
        in_specs=[SCALARS, WHOLE, WHOLE, pl.BlockSpec(memory_space=pltpu.HBM), WHOLE],
        out_specs=(WHOLE, WHOLE, WHOLE, edge_spec, edge_spec),
        out_shape=(
            jax.ShapeDtypeStruct((PX, sens * FREQ * 2, PY), BF16),
            jax.ShapeDtypeStruct((PX, COLS, PY), F32),
            jax.ShapeDtypeStruct((PX, 3, STRIP, 128), F32),
            edge,
            edge,
        ),
        scratch_shapes=[
            pltpu.VMEM((2, FREQ, per, 2, PX, PY), BF16),
            pltpu.SemaphoreType.DMA((2,)),
            pltpu.VMEM((COLS, KW), BF16),
        ],
        compiler_params=params(24),
    )(inv, gathered, freq, stored, classes)


XROWS = COLS + 16 + 3 * STRIP


def edges_body(field, strips, before, after, classes, whole_strips, x_up, x_down):
    for x in range(PX):
        for t in range(3):
            low = before[x].astype(F32)[3 * t : 3 * t + 3]
            high = after[x].astype(F32)[3 * t : 3 * t + 3]
            whole_strips[x, t] = jnp.concatenate([low, strips[x, t, 3:21, :], high], axis=0)
    for first, out in ((PX - 3, x_up), (0, x_down)):
        for j in range(3):
            x = first + j
            out[j, :COLS] = field[x].astype(BF16)
            out[j, COLS : COLS + 16] = jnp.broadcast_to(classes[x : x + 1, :], (16, PY)).astype(BF16)
            for t in range(3):
                at = COLS + 16 + t * STRIP
                out[j, at : at + STRIP] = whole_strips[x, t].astype(BF16)


def edges(field, strips, before, after, classes):
    send = jax.ShapeDtypeStruct((3, XROWS, 128), BF16)
    return pl.pallas_call(
        edges_body,
        in_specs=[WHOLE] * 5,
        out_specs=(WHOLE, pl.BlockSpec(), pl.BlockSpec()),
        out_shape=(jax.ShapeDtypeStruct((PX, 3, STRIP, 128), F32), send, send),
        compiler_params=params(8),
    )(field, strips, before, after, classes)


def table_of(labels, table):
    kappa = jnp.zeros(labels.shape, F32)
    for j in range(8):
        kappa = jnp.where(labels == float(j + 1), table[j], kappa)
    return kappa


def weights(here, up, down, left, right):
    four = [jnp.minimum(here, n) for n in (up, down, left, right)]
    return [1.0 - (four[0] + four[1] + four[2] + four[3])] + four


def smooth(value, load, axis, size):
    for turn in range(SWEEPS):
        fresh = []
        for i in range(1, len(value) - 1):
            m = load(i + turn)
            mid = value[i]
            left = pltpu.roll(mid, 1, axis)
            right = pltpu.roll(mid, size - 1, axis)
            a = m[0] * mid + m[1] * value[i - 1]
            b = m[2] * value[i + 1] + m[3] * left
            fresh.append(a + (b + m[4] * right))
        value = fresh
    return value


def sweep_body(table, field, strips, above, below, classes, prior, prior_out, main_w, strip_w):
    ext = PX + 6
    label = [above[j, COLS : COLS + 8].astype(F32) for j in range(3)]
    label += [jnp.broadcast_to(classes[x : x + 1, :], (8, PY)) for x in range(PX)]
    label += [below[j, COLS : COLS + 8].astype(F32) for j in range(3)]
    kappa = [table_of(v, table) for v in label]
    for i in range(1, ext - 1):
        k = kappa[i]
        ws = weights(k, kappa[i - 1], kappa[i + 1], pltpu.roll(k, 1, 1), pltpu.roll(k, PY - 1, 1))
        for d in range(5):
            main_w[i, d] = ws[d]
    at = COLS + 16

    def strip_rows(t):
        lo, hi = at + t * STRIP, at + (t + 1) * STRIP
        return (
            [above[j, lo:hi].astype(F32) for j in range(3)]
            + [strips[x, t] for x in range(PX)]
            + [below[j, lo:hi].astype(F32) for j in range(3)]
        )

    kappa = [table_of(v, table) for v in strip_rows(2)]
    for i in range(1, ext - 1):
        k = kappa[i]
        ws = weights(k, kappa[i - 1], kappa[i + 1], pltpu.roll(k, 1, 0), pltpu.roll(k, STRIP - 1, 0))
        for d in range(5):
            strip_w[i, d] = ws[d]
    edge = [smooth(strip_rows(t), lambda i: [strip_w[i, d] for d in range(5)], 0, STRIP) for t in range(2)]
    rows = lax.broadcasted_iota(jnp.int32, (STRIP, PY), 0)
    lanes = lax.broadcasted_iota(jnp.int32, (STRIP, PY), 1)
    pick = (strip_lane(rows) == lanes).astype(BF16)
    tn = (((0,), (0,)), ((), ()))
    for x in range(PX):
        both = jnp.concatenate([edge[0][x], edge[1][x]], axis=1).astype(BF16)
        prior[x] = lax.dot_general(both, pick, tn, preferred_element_type=F32).astype(BF16)

    def columns(g, _):
        c = pl.multiple_of(g * 16, 16)
        value = [above[j, pl.ds(c, 16), :].astype(F32) for j in range(3)]
        value += [field[x, pl.ds(c, 16), :] for x in range(PX)]
        value += [below[j, pl.ds(c, 16), :].astype(F32) for j in range(3)]

        def load(i):
            return [jnp.concatenate([main_w[i, d]] * 2, axis=0) for d in range(5)]

        value = smooth(value, load, 1, PY)
        lane = lax.broadcasted_iota(jnp.int32, (16, PY), 1)
        inner = (lane >= 3) & (lane < PY - 3)
        for x in range(PX):
            at_edge = prior[x, pl.ds(c, 16), :].astype(F32)
            prior[x, pl.ds(c, 16), :] = jnp.where(inner, value[x], at_edge).astype(BF16)
        return 0

    lax.fori_loop(0, COLS // 16, columns, 0)
    prior_out[...] = jnp.swapaxes(prior[...], 0, 1)


def sweeps(table, field, strips, above, below, classes):
    ext = PX + 6
    return pl.pallas_call(
        sweep_body,
        in_specs=[SCALARS] + [WHOLE] * 5,
        out_specs=(WHOLE, pl.BlockSpec()),
        out_shape=(
            jax.ShapeDtypeStruct((PX, COLS, PY), BF16),
            jax.ShapeDtypeStruct((COLS, PX, PY), BF16),
        ),
        scratch_shapes=[pltpu.VMEM((ext, 5, 8, PY), F32), pltpu.VMEM((ext, 5, STRIP, PY), F32)],
        compiler_params=params(12),
    )(table, field, strips, above, below, classes)


def forward_body(prior, ops, keep, send):
    group = pl.program_id(0)
    core = lax.axis_index("core")
    rows = pl.ds(pl.multiple_of(group * KW, KW), KW)
    left = jnp.concatenate([prior[x] for x in range(PX)], axis=1)
    right = jnp.concatenate([ops[x, rows, :] for x in range(PX)], axis=1)
    nt = (((1,), (1,)), ((), ()))
    total = lax.dot_general(left, right, nt, preferred_element_type=F32)
    for chip in range(8):
        even = total[chip * 32 : chip * 32 + 16]
        odd = total[chip * 32 + 16 : chip * 32 + 32]
        keep[group * 8 + chip] = jnp.where(core == 0, even, odd)
        send[group * 8 + chip] = jnp.where(core == 0, odd, even).astype(BF16)


def forward(prior, ops):
    return pl.pallas_call(
        forward_body,
        grid=(NW,),
        in_specs=[WHOLE, WHOLE],
        out_specs=(WHOLE, WHOLE),
        out_shape=(
            jax.ShapeDtypeStruct((64, 16, KW), F32),
            jax.ShapeDtypeStruct((64, 16, KW), BF16),
        ),
        compiler_params=params(16),
    )(prior, ops)


def reduced(keep, send):
    got = lax.ppermute(send, "core", [(0, 1), (1, 0)])
    chip = (keep + got.astype(F32)).astype(BF16)
    pieces = lax.all_to_all(chip, CHIPS, 0, 0, tiled=True)
    return jnp.sum(pieces.astype(F32), axis=0)


def shifted(value, axis, step):
    size = lax.axis_size(axis)
    return lax.ppermute(value, axis, [(i, i + step) for i in range(size) if 0 <= i + step < size])


def on_device(seafloor_ops, sensor_data, column_freq, row_owner, coef_class, coef_table):
    sens = seafloor_ops.shape[0]
    per, own = sensor_data.shape[0], sensor_data.shape[3]
    quad_weight = 2.0 * sens / (PX * lax.axis_size(WIDE) * PY * lax.axis_size(NARROW))
    my_freq = lax.dynamic_slice_in_dim(column_freq, lax.axis_index(NARROW) * own, own)
    mask = my_freq[None, None, None, :] == jnp.arange(FREQ, dtype=jnp.int32)[None, :, None, None]
    chosen = jnp.sum(jnp.where(mask, sensor_data, 0).astype(F32), axis=1).astype(BF16)
    block = chosen.reshape(per * 2, own).T
    sent = jnp.broadcast_to(block[None], (128,) + block.shape)
    gathered = lax.all_to_all(sent, BOTH, 0, 0, tiled=True).reshape(NW, COLS, per * 2)

    ids = jnp.arange(sens, dtype=jnp.int32)
    inverse = jnp.sum(jnp.where(row_owner[None, :] == ids[:, None], ids[None, :], 0), axis=1)
    classes = (coef_class + 1).astype(F32)

    ops, field, strips, y_up, y_down = adjoint(
        inverse, gathered, column_freq.reshape(COLS, 1), seafloor_ops, classes
    )
    before = shifted(y_up, NARROW, 1)
    after = shifted(y_down, NARROW, -1)
    strips, x_up, x_down = edges(field, strips, before, after, classes)
    above = shifted(x_up, WIDE, 1)
    below = shifted(x_down, WIDE, -1)
    prior, prior_field = sweeps(coef_table, field, strips, above, below, classes)
    total = reduced(*forward(prior, ops)) * quad_weight
    hessian = total.astype(BF16).reshape(own, FREQ, per, 2).transpose(2, 1, 3, 0)
    return hessian, prior_field


def solution(mesh):
    fine = jax.sharding.Mesh(mesh.devices.reshape(2, 4, 4, 2, 2), BOTH)
    placed = (
        P(None, None, None, WIDE, NARROW),
        P(WIDE, None, None, NARROW),
        P(),
        P(),
        P(WIDE, NARROW),
        P(),
    )
    return jax.shard_map(
        on_device,
        mesh=fine,
        in_specs=placed,
        out_specs=(P(WIDE, None, None, NARROW), P(None, WIDE, NARROW)),
        check_vma=False,
    )
```

```python
import jax
import jax.numpy as jnp
from jax import lax
from jax.experimental import pallas as pl
from jax.experimental.pallas import tpu as pltpu
from jax.sharding import PartitionSpec as P

SWEEPS = 3
WIDE, NARROW = ("z_lo", "x"), ("y", "z_hi", "core")
BOTH = WIDE + NARROW
CHIPS = WIDE + NARROW[:2]
F32 = jnp.float32
BF16 = jnp.bfloat16
WHOLE = pl.BlockSpec(memory_space=pltpu.VMEM)
SCALARS = pl.BlockSpec(memory_space=pltpu.SMEM)
PX, PY = 16, 128
COLS, FREQ, NW, KW = 256, 4, 8, 512
STRIP = 24


def params(mib):
    return pltpu.CompilerParams(vmem_limit_bytes=mib << 20)


def strip_lane(rows):
    left = (rows >= 3) & (rows < 12)
    right = (rows >= 12) & (rows < 21)
    return jnp.where(left, rows - 3, jnp.where(right, rows + (PY - 21), -1))


def adjoint_body(inv, gathered, freq, stored, classes, ops, field, strips, y_a, y_b, x_a, x_b, buf, sems, probes):
    group = pl.program_id(0)
    per = buf.shape[2]

    def fetch(which, slot):
        def one(j, _):
            sensor = inv[which * per + j]
            pltpu.make_async_copy(stored.at[sensor], buf.at[slot, :, j], sems.at[slot]).start()
            return 0

        lax.fori_loop(0, per, one, 0, unroll=8)

    @pl.when(group == 0)
    def _():
        fetch(0, 0)
        field[...] = jnp.zeros_like(field)

    @pl.when(group + 1 < pl.num_programs(0))
    def _():
        fetch(group + 1, (group + 1) % 2)

    slot = group % 2
    block = gathered[group]
    for f in range(FREQ):
        probes[:, f * 128 : f * 128 + 128] = jnp.where(freq[...] == f, block, 0).astype(BF16)
    pltpu.make_async_copy(buf.at[slot], buf.at[slot], sems.at[slot]).wait()
    for f in range(0, FREQ, 2):
        laid = jnp.swapaxes(buf[slot, f : f + 2].reshape(per * 4, PX, PY), 0, 1)
        start = pl.multiple_of(group * KW + f * per * 2, per * 4)
        ops[:, pl.ds(start, per * 4), :] = laid
        for x in range(0, PX, 2):
            pair = jnp.concatenate([laid[x], laid[x + 1]], axis=1)
            both = jnp.dot(probes[:, f * 128 : f * 128 + 256], pair, preferred_element_type=F32)
            field[x] += both[:, :PY]
            field[x + 1] += both[:, PY:]

    @pl.when(group == pl.num_programs(0) - 1)
    def _():
        line = lax.broadcasted_iota(jnp.int32, (STRIP, 2 * PY), 0)
        lanes = lax.broadcasted_iota(jnp.int32, (STRIP, 2 * PY), 1)
        pick = (strip_lane(line) == lanes % PY).astype(F32).astype(BF16)
        nt = (((1,), (1,)), ((), ()))
        for x in range(PX):
            mine = field[x]
            high = mine.astype(BF16)
            low = (mine - high.astype(F32)).astype(BF16)
            strip = lax.dot_general(pick, jnp.concatenate([high, low], axis=1), nt, preferred_element_type=F32)
            row = jnp.broadcast_to(classes[x : x + 1, :], (PY, PY)).astype(BF16)
            label = lax.dot_general(pick[:, :PY], row, nt, preferred_element_type=F32)
            parts = (strip[:, :128], strip[:, 128:], label)
            for t in range(3):
                strips[x, t] = parts[t]
            pad = jnp.zeros((7, 128), F32)
            up = jnp.concatenate([p[18:21] for p in parts] + [pad], axis=0).astype(BF16)
            down = jnp.concatenate([p[3:6] for p in parts] + [pad], axis=0).astype(BF16)
            even = lax.axis_index(NARROW[-1]) == 0
            y_a[x] = jnp.where(even, up, down)
            y_b[x] = jnp.where(even, down, up)
        even = lax.axis_index(WIDE[-1]) % 2 == 0
        for first, out in ((jnp.where(even, PX - 3, 0), x_a), (jnp.where(even, 0, PX - 3), x_b)):
            for j in range(3):
                out[j, :COLS] = field[first + j].astype(BF16)
                row = classes[pl.ds(first + j, 1), :]
                out[j, COLS : COLS + 16] = jnp.broadcast_to(row, (16, PY)).astype(BF16)


def adjoint(inv, gathered, freq, stored, classes):
    sens = stored.shape[0]
    per = sens // NW
    y_edge = jax.ShapeDtypeStruct((PX, 16, 128), BF16)
    x_edge = jax.ShapeDtypeStruct((3, COLS + 16, PY), BF16)
    return pl.pallas_call(
        adjoint_body,
        grid=(NW,),
        in_specs=[SCALARS, WHOLE, WHOLE, pl.BlockSpec(memory_space=pltpu.HBM), WHOLE],
        out_specs=(WHOLE,) * 7,
        out_shape=(
            jax.ShapeDtypeStruct((PX, sens * FREQ * 2, PY), BF16),
            jax.ShapeDtypeStruct((PX, COLS, PY), F32),
            jax.ShapeDtypeStruct((PX, 3, STRIP, 128), F32),
            y_edge,
            y_edge,
            x_edge,
            x_edge,
        ),
        scratch_shapes=[
            pltpu.VMEM((2, FREQ, per, 2, PX, PY), BF16),
            pltpu.SemaphoreType.DMA((2,)),
            pltpu.VMEM((COLS, KW), BF16),
        ],
        compiler_params=params(24),
    )(inv, gathered, freq, stored, classes)


SROWS = 80


def halves(even, first, second):
    return jnp.where(even, second, first), jnp.where(even, first, second)


def edges_body(strips, y_a, y_b, whole, s_a, s_b):
    even = lax.axis_index(NARROW[-1]) == 0
    for x in range(PX):
        low, high = halves(even, y_a[x].astype(F32), y_b[x].astype(F32))
        for t in range(3):
            at = slice(3 * t, 3 * t + 3)
            whole[x, t] = jnp.concatenate([low[at], strips[x, t, 3:21, :], high[at]], axis=0)
    even = lax.axis_index(WIDE[-1]) % 2 == 0
    pad = jnp.zeros((SROWS - 3 * STRIP, 128), F32)
    for first, out in ((jnp.where(even, PX - 3, 0), s_a), (jnp.where(even, 0, PX - 3), s_b)):
        for j in range(3):
            out[j] = jnp.concatenate([whole[first + j, t] for t in range(3)] + [pad], axis=0).astype(BF16)


def edges(strips, y_a, y_b):
    send = jax.ShapeDtypeStruct((3, SROWS, 128), BF16)
    return pl.pallas_call(
        edges_body,
        in_specs=[WHOLE] * 3,
        out_specs=(WHOLE,) * 3,
        out_shape=(jax.ShapeDtypeStruct((PX, 3, STRIP, 128), F32), send, send),
        compiler_params=params(8),
    )(strips, y_a, y_b)


def table_of(labels, table):
    kappa = jnp.zeros(labels.shape, F32)
    for j in range(8):
        kappa = jnp.where(labels == float(j + 1), table[j], kappa)
    return kappa


def weights(here, up, down, left, right):
    four = [jnp.minimum(here, n) for n in (up, down, left, right)]
    return [1.0 - (four[0] + four[1] + four[2] + four[3])] + four


def smooth(value, load, axis, size):
    for turn in range(SWEEPS):
        fresh = []
        for i in range(1, len(value) - 1):
            m = load(i + turn)
            mid = value[i]
            left = pltpu.roll(mid, 1, axis)
            right = pltpu.roll(mid, size - 1, axis)
            a = m[0] * mid + m[1] * value[i - 1]
            b = m[2] * value[i + 1] + m[3] * left
            fresh.append(a + (b + m[4] * right))
        value = fresh
    return value


def coefficients(kappa, axis, size, out):
    for i in range(1, PX + 5):
        k = kappa[i]
        ws = weights(k, kappa[i - 1], kappa[i + 1], pltpu.roll(k, 1, axis), pltpu.roll(k, size - 1, axis))
        for d in range(5):
            out[i, d] = ws[d]


def inner_body(table, field, x_a, x_b, classes, inner, coef):
    even = lax.axis_index(WIDE[-1]) % 2 == 0

    def halo(j, rows):
        return halves(even, x_a[j, rows, :].astype(F32), x_b[j, rows, :].astype(F32))

    label = [halo(j, slice(COLS, COLS + 8)) for j in range(3)]
    own = [jnp.broadcast_to(classes[x : x + 1, :], (8, PY)) for x in range(PX)]
    label = [v[0] for v in label] + own + [v[1] for v in label]
    coefficients([table_of(v, table) for v in label], 1, PY, coef)

    def columns(g, _):
        rows = pl.ds(pl.multiple_of(g * 16, 16), 16)
        ends = [halo(j, rows) for j in range(3)]
        value = [v[0] for v in ends] + [field[x, rows, :] for x in range(PX)] + [v[1] for v in ends]

        def load(i):
            return [jnp.concatenate([coef[i, d]] * 2, axis=0) for d in range(5)]

        value = smooth(value, load, 1, PY)
        for x in range(PX):
            inner[x, rows, :] = value[x].astype(BF16)
        return 0

    lax.fori_loop(0, COLS // 16, columns, 0)


def inner_sweeps(table, field, x_a, x_b, classes):
    return pl.pallas_call(
        inner_body,
        in_specs=[SCALARS] + [WHOLE] * 4,
        out_specs=WHOLE,
        out_shape=jax.ShapeDtypeStruct((PX, COLS, PY), BF16),
        scratch_shapes=[pltpu.VMEM((PX + 6, 5, 8, PY), F32)],
        compiler_params=params(12),
    )(table, field, x_a, x_b, classes)


def outer_body(table, whole, s_a, s_b, inner, prior, prior_out, coef):
    even = lax.axis_index(WIDE[-1]) % 2 == 0

    def strip_rows(t):
        rows = slice(t * STRIP, (t + 1) * STRIP)
        ends = [halves(even, s_a[j, rows, :].astype(F32), s_b[j, rows, :].astype(F32)) for j in range(3)]
        return [v[0] for v in ends] + [whole[x, t] for x in range(PX)] + [v[1] for v in ends]

    coefficients([table_of(v, table) for v in strip_rows(2)], 0, STRIP, coef)
    edge = [smooth(strip_rows(t), lambda i: [coef[i, d] for d in range(5)], 0, STRIP) for t in range(2)]
    rows = lax.broadcasted_iota(jnp.int32, (STRIP, PY), 0)
    lanes = lax.broadcasted_iota(jnp.int32, (STRIP, PY), 1)
    pick = (strip_lane(rows) == lanes).astype(F32).astype(BF16)
    lane = lax.broadcasted_iota(jnp.int32, (COLS, PY), 1)
    middle = (lane >= 3) & (lane < PY - 3)
    tn = (((0,), (0,)), ((), ()))
    for x in range(PX):
        both = jnp.concatenate([edge[0][x], edge[1][x]], axis=1).astype(BF16)
        at_edge = lax.dot_general(both, pick, tn, preferred_element_type=F32)
        prior[x] = jnp.where(middle, inner[x].astype(F32), at_edge).astype(BF16)
    prior_out[...] = jnp.swapaxes(prior[...], 0, 1)


def outer_sweeps(table, whole, s_a, s_b, inner):
    return pl.pallas_call(
        outer_body,
        in_specs=[SCALARS] + [WHOLE] * 4,
        out_specs=(WHOLE, pl.BlockSpec()),
        out_shape=(
            jax.ShapeDtypeStruct((PX, COLS, PY), BF16),
            jax.ShapeDtypeStruct((COLS, PX, PY), BF16),
        ),
        scratch_shapes=[pltpu.VMEM((PX + 6, 5, STRIP, PY), F32)],
        compiler_params=params(12),
    )(table, whole, s_a, s_b, inner)


def forward_body(prior, ops, keep, send):
    group = pl.program_id(0)
    core = lax.axis_index("core")
    rows = pl.ds(pl.multiple_of(group * KW, KW), KW)
    left = jnp.concatenate([prior[x] for x in range(PX)], axis=1)
    right = jnp.concatenate([ops[x, rows, :] for x in range(PX)], axis=1)
    nt = (((1,), (1,)), ((), ()))
    total = lax.dot_general(left, right, nt, preferred_element_type=F32)
    for chip in range(8):
        even = total[chip * 32 : chip * 32 + 16]
        odd = total[chip * 32 + 16 : chip * 32 + 32]
        keep[group * 8 + chip] = jnp.where(core == 0, even, odd)
        send[group * 8 + chip] = jnp.where(core == 0, odd, even).astype(BF16)


def forward(prior, ops):
    return pl.pallas_call(
        forward_body,
        grid=(NW,),
        in_specs=[WHOLE, WHOLE],
        out_specs=(WHOLE, WHOLE),
        out_shape=(
            jax.ShapeDtypeStruct((64, 16, KW), F32),
            jax.ShapeDtypeStruct((64, 16, KW), BF16),
        ),
        compiler_params=params(16),
    )(prior, ops)


def reduced(keep, send):
    got = lax.ppermute(send, "core", [(0, 1), (1, 0)])
    chip = (keep + got.astype(F32)).astype(BF16)
    pieces = lax.all_to_all(chip, CHIPS, 0, 0, tiled=True)
    return jnp.sum(pieces.astype(F32), axis=0)


def swapped(first, second, axis):
    size = lax.axis_size(axis)
    odd = [(i, i + 1) for i in range(1, size - 1, 2)]
    got = lax.ppermute(first, axis, [(i, i ^ 1) for i in range(size)])
    return got, lax.ppermute(second, axis, odd + [(j, i) for i, j in odd])


def on_device(seafloor_ops, sensor_data, column_freq, row_owner, coef_class, coef_table):
    sens = seafloor_ops.shape[0]
    per, own = sensor_data.shape[0], sensor_data.shape[3]
    quad_weight = 2.0 * sens / (PX * lax.axis_size(WIDE) * PY * lax.axis_size(NARROW))
    my_freq = lax.dynamic_slice_in_dim(column_freq, lax.axis_index(NARROW) * own, own)
    mask = my_freq[None, None, None, :] == jnp.arange(FREQ, dtype=jnp.int32)[None, :, None, None]
    chosen = jnp.sum(jnp.where(mask, sensor_data, 0).astype(F32), axis=1).astype(BF16)
    block = chosen.reshape(per * 2, own).T
    sent = jnp.broadcast_to(block[None], (128,) + block.shape)
    gathered = lax.all_to_all(sent, BOTH, 0, 0, tiled=True).reshape(NW, COLS, per * 2)

    ids = jnp.arange(sens, dtype=jnp.int32)
    inverse = jnp.sum(jnp.where(row_owner[None, :] == ids[:, None], ids[None, :], 0), axis=1)
    classes = (coef_class + 1).astype(F32)

    ops, field, strips, y_a, y_b, x_a, x_b = adjoint(
        inverse, gathered, column_freq.reshape(COLS, 1), seafloor_ops, classes
    )
    y_a, y_b = swapped(y_a, y_b, NARROW)
    x_a, x_b = swapped(x_a, x_b, WIDE)
    whole, s_a, s_b = edges(strips, y_a, y_b)
    s_a, s_b = swapped(s_a, s_b, WIDE)
    inner = inner_sweeps(coef_table, field, x_a, x_b, classes)
    prior, prior_field = outer_sweeps(coef_table, whole, s_a, s_b, inner)
    total = reduced(*forward(prior, ops)) * quad_weight
    hessian = total.astype(BF16).reshape(own, FREQ, per, 2).transpose(2, 1, 3, 0)
    return hessian, prior_field


def solution(mesh):
    fine = jax.sharding.Mesh(mesh.devices.reshape(2, 4, 4, 2, 2), BOTH)
    placed = (
        P(None, None, None, WIDE, NARROW),
        P(WIDE, None, None, NARROW),
        P(),
        P(),
        P(WIDE, NARROW),
        P(),
    )
    return jax.shard_map(
        on_device,
        mesh=fine,
        in_specs=placed,
        out_specs=(P(WIDE, None, None, NARROW), P(None, WIDE, NARROW)),
        check_vma=False,
    )
```

```python
import functools

import jax
import jax.numpy as jnp
from jax import lax
from jax.experimental import pallas as pl
from jax.experimental.pallas import tpu as pltpu
from jax.sharding import PartitionSpec as P


SWEEPS = 3
WIDE, NARROW = ("z_lo", "x"), ("y", "z_hi", "core")
BOTH = WIDE + NARROW
CHIPS = WIDE + NARROW[:2]
F32 = jnp.float32
BF16 = jnp.bfloat16
WHOLE = pl.BlockSpec(memory_space=pltpu.VMEM)
SCALARS = pl.BlockSpec(memory_space=pltpu.SMEM)
PX, PY = 16, 128
COLS, FREQ, NW, KW = 256, 4, 8, 512
STRIP = 24


def params(mib):
    return pltpu.CompilerParams(vmem_limit_bytes=mib << 20)


def choose_body(column_freq, data, out):
    own = data.shape[2]
    narrow = (lax.axis_index("y") * 2 + lax.axis_index("z_hi")) * 2 + lax.axis_index("core")
    shape = (own, 2 * data.shape[3])
    column = lax.broadcasted_iota(jnp.int32, shape, 0)
    freq = jnp.zeros(shape, jnp.int32)
    for j in range(own):
        freq = jnp.where(column == j, column_freq[narrow * own + j], freq)
    block = jnp.zeros(shape, F32)
    for f in range(FREQ):
        both = jnp.concatenate([data[f, 0], data[f, 1]], axis=1).astype(F32)
        block = jnp.where(freq == f, both, block)
    out[...] = jnp.broadcast_to(block.astype(BF16)[None], out.shape)


def choose(column_freq, data, receivers):
    return pl.pallas_call(
        choose_body,
        in_specs=[SCALARS, WHOLE],
        out_specs=pl.BlockSpec(),
        out_shape=jax.ShapeDtypeStruct((receivers, data.shape[2], 2 * data.shape[3]), BF16),
        compiler_params=params(8),
    )(column_freq, data)


def strip_lane(rows):
    left = (rows >= 3) & (rows < 12)
    right = (rows >= 12) & (rows < 21)
    return jnp.where(left, rows - 3, jnp.where(right, rows + (PY - 21), -1))


def adjoint_body(inv, gathered, freq, stored, classes, ops, field, strips, y_a, y_b, x_a, x_b, buf, sems, probes):
    group = pl.program_id(0)
    per = buf.shape[3]

    def fetch(which, slot):
        def one(j, _):
            sensor = inv[which * per + j]
            pltpu.make_async_copy(stored.at[sensor], buf.at[slot, :, :, j], sems.at[slot]).start()
            return 0

        lax.fori_loop(0, per, one, 0, unroll=8)

    @pl.when(group == 0)
    def _():
        fetch(0, 0)
        field[...] = jnp.zeros_like(field)

    @pl.when(group + 1 < pl.num_programs(0))
    def _():
        fetch(group + 1, (group + 1) % 2)

    slot = group % 2
    block = gathered[group]
    for f in range(FREQ):
        probes[:, f * 128 : f * 128 + 128] = jnp.where(freq[...] == f, block, 0).astype(BF16)
    pltpu.make_async_copy(buf.at[slot], buf.at[slot], sems.at[slot]).wait()
    for f in range(0, FREQ, 2):
        laid = jnp.swapaxes(buf[slot, f : f + 2].reshape(per * 4, PX, PY), 0, 1)
        start = pl.multiple_of(group * KW + f * per * 2, per * 4)
        ops[:, pl.ds(start, per * 4), :] = laid
        for x in range(0, PX, 2):
            pair = jnp.concatenate([laid[x], laid[x + 1]], axis=1)
            both = jnp.dot(probes[:, f * 128 : f * 128 + 256], pair, preferred_element_type=F32)
            field[x] += both[:, :PY]
            field[x + 1] += both[:, PY:]

    @pl.when(group == pl.num_programs(0) - 1)
    def _():
        line = lax.broadcasted_iota(jnp.int32, (STRIP, 2 * PY), 0)
        lanes = lax.broadcasted_iota(jnp.int32, (STRIP, 2 * PY), 1)
        pick = (strip_lane(line) == lanes % PY).astype(F32).astype(BF16)
        nt = (((1,), (1,)), ((), ()))
        for x in range(PX):
            mine = field[x]
            high = mine.astype(BF16)
            low = (mine - high.astype(F32)).astype(BF16)
            strip = lax.dot_general(pick, jnp.concatenate([high, low], axis=1), nt, preferred_element_type=F32)
            row = jnp.broadcast_to(classes[x : x + 1, :], (PY, PY)).astype(BF16)
            label = lax.dot_general(pick[:, :PY], row, nt, preferred_element_type=F32)
            parts = (strip[:, :128], strip[:, 128:], label)
            for t in range(3):
                strips[x, t] = parts[t]
            pad = jnp.zeros((7, 128), F32)
            up = jnp.concatenate([p[18:21] for p in parts] + [pad], axis=0).astype(BF16)
            down = jnp.concatenate([p[3:6] for p in parts] + [pad], axis=0).astype(BF16)
            even = lax.axis_index(NARROW[-1]) == 0
            y_a[x] = jnp.where(even, up, down)
            y_b[x] = jnp.where(even, down, up)
        even = lax.axis_index(WIDE[-1]) % 2 == 0
        for first, out in ((jnp.where(even, PX - 3, 0), x_a), (jnp.where(even, 0, PX - 3), x_b)):
            for j in range(3):
                out[j, :COLS] = field[first + j].astype(BF16)
                row = classes[pl.ds(first + j, 1), :]
                out[j, COLS : COLS + 16] = jnp.broadcast_to(row, (16, PY)).astype(BF16)


def adjoint(inv, gathered, freq, stored, classes):
    sens = stored.shape[0]
    per = sens // NW
    y_edge = jax.ShapeDtypeStruct((PX, 16, 128), BF16)
    x_edge = jax.ShapeDtypeStruct((3, COLS + 16, PY), BF16)
    return pl.pallas_call(
        adjoint_body,
        grid=(NW,),
        in_specs=[SCALARS, WHOLE, WHOLE, pl.BlockSpec(memory_space=pltpu.HBM), WHOLE],
        out_specs=(WHOLE,) * 7,
        out_shape=(
            jax.ShapeDtypeStruct((PX, sens * FREQ * 2, PY), BF16),
            jax.ShapeDtypeStruct((PX, COLS, PY), F32),
            jax.ShapeDtypeStruct((PX, 3, STRIP, 128), F32),
            y_edge,
            y_edge,
            x_edge,
            x_edge,
        ),
        scratch_shapes=[
            pltpu.VMEM((2, FREQ, 2, per, PX, PY), BF16),
            pltpu.SemaphoreType.DMA((2,)),
            pltpu.VMEM((COLS, KW), BF16),
        ],
        compiler_params=params(24),
    )(inv, gathered, freq, stored, classes)


SROWS = 80


def halves(even, first, second):
    return jnp.where(even, second, first), jnp.where(even, first, second)


def edges_body(strips, y_a, y_b, whole, s_a, s_b):
    even = lax.axis_index(NARROW[-1]) == 0
    for x in range(PX):
        low, high = halves(even, y_a[x].astype(F32), y_b[x].astype(F32))
        for t in range(3):
            at = slice(3 * t, 3 * t + 3)
            whole[x, t] = jnp.concatenate([low[at], strips[x, t, 3:21, :], high[at]], axis=0)
    even = lax.axis_index(WIDE[-1]) % 2 == 0
    pad = jnp.zeros((SROWS - 3 * STRIP, 128), F32)
    for first, out in ((jnp.where(even, PX - 3, 0), s_a), (jnp.where(even, 0, PX - 3), s_b)):
        for j in range(3):
            out[j] = jnp.concatenate([whole[first + j, t] for t in range(3)] + [pad], axis=0).astype(BF16)


def edges(strips, y_a, y_b):
    send = jax.ShapeDtypeStruct((3, SROWS, 128), BF16)
    return pl.pallas_call(
        edges_body,
        in_specs=[WHOLE] * 3,
        out_specs=(WHOLE,) * 3,
        out_shape=(jax.ShapeDtypeStruct((PX, 3, STRIP, 128), F32), send, send),
        compiler_params=params(8),
    )(strips, y_a, y_b)


def table_of(labels, table):
    kappa = jnp.zeros(labels.shape, F32)
    for j in range(8):
        kappa = jnp.where(labels == float(j + 1), table[j], kappa)
    return kappa


def weights(here, up, down, left, right):
    four = [jnp.minimum(here, n) for n in (up, down, left, right)]
    return [1.0 - (four[0] + four[1] + four[2] + four[3])] + four


def smooth(value, load, axis, size):
    for turn in range(SWEEPS):
        fresh = []
        for i in range(1, len(value) - 1):
            m = load(i + turn)
            mid = value[i]
            left = pltpu.roll(mid, 1, axis)
            right = pltpu.roll(mid, size - 1, axis)
            a = m[0] * mid + m[1] * value[i - 1]
            b = m[2] * value[i + 1] + m[3] * left
            fresh.append(a + (b + m[4] * right))
        value = fresh
    return value


def coefficients(kappa, axis, size, out):
    for i in range(1, PX + 5):
        k = kappa[i]
        ws = weights(k, kappa[i - 1], kappa[i + 1], pltpu.roll(k, 1, axis), pltpu.roll(k, size - 1, axis))
        for d in range(5):
            out[i, d] = ws[d]


def inner_body(table, field, x_a, x_b, classes, inner, coef):
    even = lax.axis_index(WIDE[-1]) % 2 == 0

    def halo(j, rows):
        return halves(even, x_a[j, rows, :].astype(F32), x_b[j, rows, :].astype(F32))

    label = [halo(j, slice(COLS, COLS + 8)) for j in range(3)]
    own = [jnp.broadcast_to(classes[x : x + 1, :], (8, PY)) for x in range(PX)]
    label = [v[0] for v in label] + own + [v[1] for v in label]
    coefficients([table_of(v, table) for v in label], 1, PY, coef)

    def columns(g, _):
        rows = pl.ds(pl.multiple_of(g * 16, 16), 16)
        ends = [halo(j, rows) for j in range(3)]
        value = [v[0] for v in ends] + [field[x, rows, :] for x in range(PX)] + [v[1] for v in ends]

        def load(i):
            return [jnp.concatenate([coef[i, d]] * 2, axis=0) for d in range(5)]

        value = smooth(value, load, 1, PY)
        for x in range(PX):
            inner[x, rows, :] = value[x].astype(BF16)
        return 0

    lax.fori_loop(0, COLS // 16, columns, 0)


def inner_sweeps(table, field, x_a, x_b, classes):
    return pl.pallas_call(
        inner_body,
        in_specs=[SCALARS] + [WHOLE] * 4,
        out_specs=WHOLE,
        out_shape=jax.ShapeDtypeStruct((PX, COLS, PY), BF16),
        scratch_shapes=[pltpu.VMEM((PX + 6, 5, 8, PY), F32)],
        compiler_params=params(12),
    )(table, field, x_a, x_b, classes)


def outer_body(table, whole, s_a, s_b, inner, prior, prior_out, coef):
    even = lax.axis_index(WIDE[-1]) % 2 == 0

    def strip_rows(t):
        rows = slice(t * STRIP, (t + 1) * STRIP)
        ends = [halves(even, s_a[j, rows, :].astype(F32), s_b[j, rows, :].astype(F32)) for j in range(3)]
        return [v[0] for v in ends] + [whole[x, t] for x in range(PX)] + [v[1] for v in ends]

    coefficients([table_of(v, table) for v in strip_rows(2)], 0, STRIP, coef)
    edge = [smooth(strip_rows(t), lambda i: [coef[i, d] for d in range(5)], 0, STRIP) for t in range(2)]
    rows = lax.broadcasted_iota(jnp.int32, (STRIP, PY), 0)
    lanes = lax.broadcasted_iota(jnp.int32, (STRIP, PY), 1)
    pick = (strip_lane(rows) == lanes).astype(F32).astype(BF16)
    lane = lax.broadcasted_iota(jnp.int32, (COLS, PY), 1)
    middle = (lane >= 3) & (lane < PY - 3)
    tn = (((0,), (0,)), ((), ()))
    for x in range(PX):
        both = jnp.concatenate([edge[0][x], edge[1][x]], axis=1).astype(BF16)
        at_edge = lax.dot_general(both, pick, tn, preferred_element_type=F32)
        prior[x] = jnp.where(middle, inner[x].astype(F32), at_edge).astype(BF16)
    prior_out[...] = jnp.swapaxes(prior[...], 0, 1)


def outer_sweeps(table, whole, s_a, s_b, inner):
    return pl.pallas_call(
        outer_body,
        in_specs=[SCALARS] + [WHOLE] * 4,
        out_specs=(WHOLE, pl.BlockSpec()),
        out_shape=(
            jax.ShapeDtypeStruct((PX, COLS, PY), BF16),
            jax.ShapeDtypeStruct((COLS, PX, PY), BF16),
        ),
        scratch_shapes=[pltpu.VMEM((PX + 6, 5, STRIP, PY), F32)],
        compiler_params=params(12),
    )(table, whole, s_a, s_b, inner)


def forward_body(prior, ops, keep, send):
    group = pl.program_id(0)
    core = lax.axis_index("core")
    rows = pl.ds(pl.multiple_of(group * KW, KW), KW)
    left = jnp.concatenate([prior[x] for x in range(PX)], axis=1)
    right = jnp.concatenate([ops[x, rows, :] for x in range(PX)], axis=1)
    nt = (((1,), (1,)), ((), ()))
    total = lax.dot_general(left, right, nt, preferred_element_type=F32)
    for chip in range(8):
        even = total[chip * 32 : chip * 32 + 16]
        odd = total[chip * 32 + 16 : chip * 32 + 32]
        keep[group * 8 + chip] = jnp.where(core == 0, even, odd)
        send[group * 8 + chip] = jnp.where(core == 0, odd, even).astype(BF16)


def forward(prior, ops):
    return pl.pallas_call(
        forward_body,
        grid=(NW,),
        in_specs=[WHOLE, WHOLE],
        out_specs=(WHOLE, WHOLE),
        out_shape=(
            jax.ShapeDtypeStruct((64, 16, KW), F32),
            jax.ShapeDtypeStruct((64, 16, KW), BF16),
        ),
        compiler_params=params(16),
    )(prior, ops)


def total_body(pieces, out, *, weight):
    total = pieces[0].astype(F32)
    for chip in range(1, pieces.shape[0]):
        total = total + pieces[chip].astype(F32)
    total = (total * weight).astype(BF16)
    rows = out.shape[3]
    for f in range(FREQ):
        for q in range(2):
            at = (f * 2 + q) * rows
            out[f, q] = total[:, at : at + rows]


def reduced(keep, send, weight):
    got = lax.ppermute(send, "core", [(0, 1), (1, 0)])
    chip = (keep + got.astype(F32)).astype(BF16)
    pieces = lax.all_to_all(chip, CHIPS, 0, 0, tiled=True)
    return pl.pallas_call(
        functools.partial(total_body, weight=weight),
        in_specs=[WHOLE],
        out_specs=pl.BlockSpec(),
        out_shape=jax.ShapeDtypeStruct((FREQ, 2, pieces.shape[1], KW // (FREQ * 2)), BF16),
        compiler_params=params(8),
    )(pieces)


def swapped(first, second, axis):
    size = lax.axis_size(axis)
    odd = [(i, i + 1) for i in range(1, size - 1, 2)]
    far = lax.ppermute(second, axis, odd + [(j, i) for i, j in odd])
    near = lax.ppermute(first, axis, [(i, i ^ 1) for i in range(size)])
    return near, far


def on_device(seafloor_ops, sensor_data, column_freq, row_owner, coef_class, coef_table):
    sens = seafloor_ops.shape[0]
    per = sensor_data.shape[0]
    quad_weight = 2.0 * sens / (PX * lax.axis_size(WIDE) * PY * lax.axis_size(NARROW))
    sent = choose(column_freq, sensor_data.transpose(1, 2, 3, 0), lax.axis_size(BOTH))
    gathered = lax.all_to_all(sent, BOTH, 0, 0, tiled=True).reshape(NW, COLS, per * 2)

    ids = jnp.arange(sens, dtype=jnp.int32)
    inverse = jnp.sum(jnp.where(row_owner[None, :] == ids[:, None], ids[None, :], 0), axis=1)
    classes = (coef_class + 1).astype(F32)

    ops, field, strips, y_a, y_b, x_a, x_b = adjoint(
        inverse, gathered, column_freq.reshape(COLS, 1), seafloor_ops, classes
    )
    y_a, y_b = swapped(y_a, y_b, NARROW)
    x_a, x_b = swapped(x_a, x_b, WIDE)
    whole, s_a, s_b = edges(strips, y_a, y_b)
    s_a, s_b = swapped(s_a, s_b, WIDE)
    inner = inner_sweeps(coef_table, field, x_a, x_b, classes)
    prior, prior_field = outer_sweeps(coef_table, whole, s_a, s_b, inner)
    hessian = reduced(*forward(prior, ops), quad_weight).transpose(3, 0, 1, 2)
    return hessian, prior_field


def solution(mesh):
    fine = jax.sharding.Mesh(mesh.devices.reshape(2, 4, 4, 2, 2), BOTH)
    placed = (
        P(None, None, None, WIDE, NARROW),
        P(WIDE, None, None, NARROW),
        P(),
        P(),
        P(WIDE, NARROW),
        P(),
    )
    return jax.shard_map(
        on_device,
        mesh=fine,
        in_specs=placed,
        out_specs=(P(WIDE, None, None, NARROW), P(None, WIDE, NARROW)),
        check_vma=False,
    )
```

```python
import functools

import jax
import jax.numpy as jnp
from jax import lax
from jax.experimental import pallas as pl
from jax.experimental.pallas import tpu as pltpu
from jax.sharding import PartitionSpec as P


SWEEPS = 3
WIDE, NARROW = ("z_lo", "x"), ("y", "z_hi", "core")
BOTH = WIDE + NARROW
CHIPS = WIDE + NARROW[:2]
F32 = jnp.float32
BF16 = jnp.bfloat16
WHOLE = pl.BlockSpec(memory_space=pltpu.VMEM)
SCALARS = pl.BlockSpec(memory_space=pltpu.SMEM)
PX, PY = 16, 128
COLS, FREQ, NW, KW = 256, 4, 8, 512
STRIP = 24


def params(mib):
    return pltpu.CompilerParams(vmem_limit_bytes=mib << 20)


def choose_body(column_freq, data, out):
    own = data.shape[2]
    narrow = (lax.axis_index("y") * 2 + lax.axis_index("z_hi")) * 2 + lax.axis_index("core")
    shape = (own, 2 * data.shape[3])
    column = lax.broadcasted_iota(jnp.int32, shape, 0)
    freq = jnp.zeros(shape, jnp.int32)
    for j in range(own):
        freq = jnp.where(column == j, column_freq[narrow * own + j], freq)
    block = jnp.zeros(shape, F32)
    for f in range(FREQ):
        both = jnp.concatenate([data[f, 0], data[f, 1]], axis=1).astype(F32)
        block = jnp.where(freq == f, both, block)
    out[...] = jnp.broadcast_to(block.astype(BF16)[None], out.shape)


def choose(column_freq, data, receivers):
    return pl.pallas_call(
        choose_body,
        in_specs=[SCALARS, WHOLE],
        out_specs=pl.BlockSpec(),
        out_shape=jax.ShapeDtypeStruct((receivers, data.shape[2], 2 * data.shape[3]), BF16),
        compiler_params=params(8),
    )(column_freq, data)


def strip_lane(rows):
    left = (rows >= 3) & (rows < 12)
    right = (rows >= 12) & (rows < 21)
    return jnp.where(left, rows - 3, jnp.where(right, rows + (PY - 21), -1))


def adjoint_body(inv, gathered, freq, stored, classes, ops, field, strips, y_a, y_b, x_a, x_b, buf, sems, probes, masks):
    group = pl.program_id(0)
    per = buf.shape[3]

    def fetch(which, slot):
        def one(j, _):
            sensor = inv[which * per + j]
            pltpu.make_async_copy(stored.at[sensor], buf.at[slot, :, :, j], sems.at[slot]).start()
            return 0

        lax.fori_loop(0, per, one, 0, unroll=8)

    @pl.when(group == 0)
    def _():
        fetch(0, 0)
        field[...] = jnp.zeros_like(field)
        for f in range(FREQ):
            masks[f] = jnp.broadcast_to((freq[...] == f).astype(F32), (COLS, 128)).astype(BF16)

    @pl.when(group + 1 < pl.num_programs(0))
    def _():
        fetch(group + 1, (group + 1) % 2)

    slot = group % 2
    block = gathered[group]
    for f in range(FREQ):
        probes[:, f * 128 : f * 128 + 128] = block * masks[f]
    pltpu.make_async_copy(buf.at[slot], buf.at[slot], sems.at[slot]).wait()
    for f in range(0, FREQ, 2):
        laid = jnp.swapaxes(buf[slot, f : f + 2].reshape(per * 4, PX, PY), 0, 1)
        start = pl.multiple_of(group * KW + f * per * 2, per * 4)
        ops[:, pl.ds(start, per * 4), :] = laid
        for x in range(0, PX, 2):
            pair = jnp.concatenate([laid[x], laid[x + 1]], axis=1)
            both = jnp.dot(probes[:, f * 128 : f * 128 + 256], pair, preferred_element_type=F32)
            field[x] += both[:, :PY]
            field[x + 1] += both[:, PY:]

    @pl.when(group == pl.num_programs(0) - 1)
    def _():
        line = lax.broadcasted_iota(jnp.int32, (STRIP, 2 * PY), 0)
        lanes = lax.broadcasted_iota(jnp.int32, (STRIP, 2 * PY), 1)
        pick = (strip_lane(line) == lanes % PY).astype(F32).astype(BF16)
        nt = (((1,), (1,)), ((), ()))
        for x in range(PX):
            mine = field[x]
            high = mine.astype(BF16)
            low = (mine - high.astype(F32)).astype(BF16)
            strip = lax.dot_general(pick, jnp.concatenate([high, low], axis=1), nt, preferred_element_type=F32)
            row = jnp.broadcast_to(classes[x : x + 1, :], (PY, PY)).astype(BF16)
            label = lax.dot_general(pick[:, :PY], row, nt, preferred_element_type=F32)
            parts = (strip[:, :128], strip[:, 128:], label)
            for t in range(3):
                strips[x, t] = parts[t]
            pad = jnp.zeros((7, 128), F32)
            up = jnp.concatenate([p[18:21] for p in parts] + [pad], axis=0).astype(BF16)
            down = jnp.concatenate([p[3:6] for p in parts] + [pad], axis=0).astype(BF16)
            even = lax.axis_index(NARROW[-1]) == 0
            y_a[x] = jnp.where(even, up, down)
            y_b[x] = jnp.where(even, down, up)
        even = lax.axis_index(WIDE[-1]) % 2 == 0
        for first, out in ((jnp.where(even, PX - 3, 0), x_a), (jnp.where(even, 0, PX - 3), x_b)):
            for j in range(3):
                out[j, :COLS] = field[first + j].astype(BF16)
                row = classes[pl.ds(first + j, 1), :]
                out[j, COLS : COLS + 16] = jnp.broadcast_to(row, (16, PY)).astype(BF16)


def adjoint(inv, gathered, freq, stored, classes):
    sens = stored.shape[0]
    per = sens // NW
    y_edge = jax.ShapeDtypeStruct((PX, 16, 128), BF16)
    x_edge = jax.ShapeDtypeStruct((3, COLS + 16, PY), BF16)
    return pl.pallas_call(
        adjoint_body,
        grid=(NW,),
        in_specs=[SCALARS, WHOLE, WHOLE, pl.BlockSpec(memory_space=pltpu.HBM), WHOLE],
        out_specs=(WHOLE,) * 7,
        out_shape=(
            jax.ShapeDtypeStruct((PX, sens * FREQ * 2, PY), BF16),
            jax.ShapeDtypeStruct((PX, COLS, PY), F32),
            jax.ShapeDtypeStruct((PX, 3, STRIP, 128), F32),
            y_edge,
            y_edge,
            x_edge,
            x_edge,
        ),
        scratch_shapes=[
            pltpu.VMEM((2, FREQ, 2, per, PX, PY), BF16),
            pltpu.SemaphoreType.DMA((2,)),
            pltpu.VMEM((COLS, KW), BF16),
            pltpu.VMEM((FREQ, COLS, 128), BF16),
        ],
        compiler_params=params(24),
    )(inv, gathered, freq, stored, classes)


SROWS = 80


def halves(even, first, second):
    return jnp.where(even, second, first), jnp.where(even, first, second)


def edges_body(strips, y_a, y_b, whole, s_a, s_b):
    even = lax.axis_index(NARROW[-1]) == 0
    for x in range(PX):
        low, high = halves(even, y_a[x].astype(F32), y_b[x].astype(F32))
        for t in range(3):
            at = slice(3 * t, 3 * t + 3)
            whole[x, t] = jnp.concatenate([low[at], strips[x, t, 3:21, :], high[at]], axis=0)
    even = lax.axis_index(WIDE[-1]) % 2 == 0
    pad = jnp.zeros((SROWS - 3 * STRIP, 128), F32)
    for first, out in ((jnp.where(even, PX - 3, 0), s_a), (jnp.where(even, 0, PX - 3), s_b)):
        for j in range(3):
            out[j] = jnp.concatenate([whole[first + j, t] for t in range(3)] + [pad], axis=0).astype(BF16)


def edges(strips, y_a, y_b):
    send = jax.ShapeDtypeStruct((3, SROWS, 128), BF16)
    return pl.pallas_call(
        edges_body,
        in_specs=[WHOLE] * 3,
        out_specs=(WHOLE,) * 3,
        out_shape=(jax.ShapeDtypeStruct((PX, 3, STRIP, 128), F32), send, send),
        compiler_params=params(8),
    )(strips, y_a, y_b)


def table_of(labels, table):
    kappa = jnp.zeros(labels.shape, F32)
    for j in range(8):
        kappa = jnp.where(labels == float(j + 1), table[j], kappa)
    return kappa


def weights(here, up, down, left, right):
    four = [jnp.minimum(here, n) for n in (up, down, left, right)]
    return [1.0 - (four[0] + four[1] + four[2] + four[3])] + four


def smooth(value, load, axis, size):
    for turn in range(SWEEPS):
        fresh = []
        for i in range(1, len(value) - 1):
            m = load(i + turn)
            mid = value[i]
            left = pltpu.roll(mid, 1, axis)
            right = pltpu.roll(mid, size - 1, axis)
            a = m[0] * mid + m[1] * value[i - 1]
            b = m[2] * value[i + 1] + m[3] * left
            fresh.append(a + (b + m[4] * right))
        value = fresh
    return value


def coefficients(kappa, axis, size, out):
    for i in range(1, PX + 5):
        k = kappa[i]
        ws = weights(k, kappa[i - 1], kappa[i + 1], pltpu.roll(k, 1, axis), pltpu.roll(k, size - 1, axis))
        for d in range(5):
            out[i, d] = ws[d]


def inner_body(table, field, x_a, x_b, classes, inner, coef):
    even = lax.axis_index(WIDE[-1]) % 2 == 0

    def halo(j, rows):
        return halves(even, x_a[j, rows, :].astype(F32), x_b[j, rows, :].astype(F32))

    label = [halo(j, slice(COLS, COLS + 8)) for j in range(3)]
    own = [jnp.broadcast_to(classes[x : x + 1, :], (8, PY)) for x in range(PX)]
    label = [v[0] for v in label] + own + [v[1] for v in label]
    coefficients([table_of(v, table) for v in label], 1, PY, coef)

    def columns(g, _):
        rows = pl.ds(pl.multiple_of(g * 16, 16), 16)
        ends = [halo(j, rows) for j in range(3)]
        value = [v[0] for v in ends] + [field[x, rows, :] for x in range(PX)] + [v[1] for v in ends]

        def load(i):
            return [jnp.concatenate([coef[i, d]] * 2, axis=0) for d in range(5)]

        value = smooth(value, load, 1, PY)
        for x in range(PX):
            inner[x, rows, :] = value[x].astype(BF16)
        return 0

    lax.fori_loop(0, COLS // 16, columns, 0)


def inner_sweeps(table, field, x_a, x_b, classes):
    return pl.pallas_call(
        inner_body,
        in_specs=[SCALARS] + [WHOLE] * 4,
        out_specs=WHOLE,
        out_shape=jax.ShapeDtypeStruct((PX, COLS, PY), BF16),
        scratch_shapes=[pltpu.VMEM((PX + 6, 5, 8, PY), F32)],
        compiler_params=params(12),
    )(table, field, x_a, x_b, classes)


def outer_body(table, whole, s_a, s_b, inner, prior, coef):
    even = lax.axis_index(WIDE[-1]) % 2 == 0

    def strip_rows(t):
        rows = slice(t * STRIP, (t + 1) * STRIP)
        ends = [halves(even, s_a[j, rows, :].astype(F32), s_b[j, rows, :].astype(F32)) for j in range(3)]
        return [v[0] for v in ends] + [whole[x, t] for x in range(PX)] + [v[1] for v in ends]

    coefficients([table_of(v, table) for v in strip_rows(2)], 0, STRIP, coef)
    edge = [smooth(strip_rows(t), lambda i: [coef[i, d] for d in range(5)], 0, STRIP) for t in range(2)]
    rows = lax.broadcasted_iota(jnp.int32, (STRIP, PY), 0)
    lanes = lax.broadcasted_iota(jnp.int32, (STRIP, PY), 1)
    pick = (strip_lane(rows) == lanes).astype(F32).astype(BF16)
    lane = lax.broadcasted_iota(jnp.int32, (COLS, PY), 1)
    middle = (lane >= 3) & (lane < PY - 3)
    tn = (((0,), (0,)), ((), ()))
    for x in range(PX):
        both = jnp.concatenate([edge[0][x], edge[1][x]], axis=1).astype(BF16)
        at_edge = lax.dot_general(both, pick, tn, preferred_element_type=F32)
        prior[x] = jnp.where(middle, inner[x].astype(F32), at_edge).astype(BF16)


def outer_sweeps(table, whole, s_a, s_b, inner):
    return pl.pallas_call(
        outer_body,
        in_specs=[SCALARS] + [WHOLE] * 4,
        out_specs=WHOLE,
        out_shape=jax.ShapeDtypeStruct((PX, COLS, PY), BF16),
        scratch_shapes=[pltpu.VMEM((PX + 6, 5, STRIP, PY), F32)],
        compiler_params=params(12),
    )(table, whole, s_a, s_b, inner)


def forward_body(prior, ops, keep, send, prior_out):
    group = pl.program_id(0)
    core = lax.axis_index("core")
    rows = pl.ds(pl.multiple_of(group * KW, KW), KW)
    left = jnp.concatenate([prior[x] for x in range(PX)], axis=1)
    right = jnp.concatenate([ops[x, rows, :] for x in range(PX)], axis=1)
    nt = (((1,), (1,)), ((), ()))
    total = lax.dot_general(left, right, nt, preferred_element_type=F32)
    own = prior_out.shape[0]
    columns = pl.ds(pl.multiple_of(group * own, own), own)
    prior_out[...] = jnp.swapaxes(prior[:, columns, :], 0, 1)
    for chip in range(8):
        even = total[chip * 32 : chip * 32 + 16]
        odd = total[chip * 32 + 16 : chip * 32 + 32]
        keep[group * 8 + chip] = jnp.where(core == 0, even, odd)
        send[group * 8 + chip] = jnp.where(core == 0, odd, even).astype(BF16)


def forward(prior, ops):
    return pl.pallas_call(
        forward_body,
        grid=(NW,),
        in_specs=[WHOLE, WHOLE],
        out_specs=(WHOLE, WHOLE, pl.BlockSpec((COLS // NW, PX, PY), lambda i: (i, 0, 0))),
        out_shape=(
            jax.ShapeDtypeStruct((64, 16, KW), F32),
            jax.ShapeDtypeStruct((64, 16, KW), BF16),
            jax.ShapeDtypeStruct((COLS, PX, PY), BF16),
        ),
        compiler_params=params(16),
    )(prior, ops)


def total_body(pieces, out, *, weight):
    total = pieces[0].astype(F32)
    for chip in range(1, pieces.shape[0]):
        total = total + pieces[chip].astype(F32)
    total = (total * weight).astype(BF16)
    rows = out.shape[3]
    for f in range(FREQ):
        for q in range(2):
            at = (f * 2 + q) * rows
            out[f, q] = total[:, at : at + rows]


def reduced(keep, send, weight):
    got = lax.ppermute(send, "core", [(0, 1), (1, 0)])
    chip = (keep + got.astype(F32)).astype(BF16)
    pieces = lax.all_to_all(chip, CHIPS, 0, 0, tiled=True)
    return pl.pallas_call(
        functools.partial(total_body, weight=weight),
        in_specs=[WHOLE],
        out_specs=pl.BlockSpec(),
        out_shape=jax.ShapeDtypeStruct((FREQ, 2, pieces.shape[1], KW // (FREQ * 2)), BF16),
        compiler_params=params(8),
    )(pieces)


def swapped(first, second, axis):
    size = lax.axis_size(axis)
    odd = [(i, i + 1) for i in range(1, size - 1, 2)]
    far = lax.ppermute(second, axis, odd + [(j, i) for i, j in odd])
    near = lax.ppermute(first, axis, [(i, i ^ 1) for i in range(size)])
    return near, far


def on_device(seafloor_ops, sensor_data, column_freq, row_owner, coef_class, coef_table):
    sens = seafloor_ops.shape[0]
    per = sensor_data.shape[0]
    quad_weight = 2.0 * sens / (PX * lax.axis_size(WIDE) * PY * lax.axis_size(NARROW))
    sent = choose(column_freq, sensor_data.transpose(1, 2, 3, 0), lax.axis_size(BOTH))
    gathered = lax.all_to_all(sent, BOTH, 0, 0, tiled=True).reshape(NW, COLS, per * 2)

    ids = jnp.arange(sens, dtype=jnp.int32)
    inverse = jnp.sum(jnp.where(row_owner[None, :] == ids[:, None], ids[None, :], 0), axis=1)
    classes = (coef_class + 1).astype(F32)

    ops, field, strips, y_a, y_b, x_a, x_b = adjoint(
        inverse, gathered, column_freq.reshape(COLS, 1), seafloor_ops, classes
    )
    y_a, y_b = swapped(y_a, y_b, NARROW)
    x_a, x_b = swapped(x_a, x_b, WIDE)
    whole, s_a, s_b = edges(strips, y_a, y_b)
    s_a, s_b = swapped(s_a, s_b, WIDE)
    inner = inner_sweeps(coef_table, field, x_a, x_b, classes)
    prior = outer_sweeps(coef_table, whole, s_a, s_b, inner)
    keep, send, prior_field = forward(prior, ops)
    hessian = reduced(keep, send, quad_weight).transpose(3, 0, 1, 2)
    return hessian, prior_field


def solution(mesh):
    fine = jax.sharding.Mesh(mesh.devices.reshape(2, 4, 4, 2, 2), BOTH)
    placed = (
        P(None, None, None, WIDE, NARROW),
        P(WIDE, None, None, NARROW),
        P(),
        P(),
        P(WIDE, NARROW),
        P(),
    )
    return jax.shard_map(
        on_device,
        mesh=fine,
        in_specs=placed,
        out_specs=(P(WIDE, None, None, NARROW), P(None, WIDE, NARROW)),
        check_vma=False,
    )
```

```python
import functools

import jax
import jax.numpy as jnp
from jax import lax
from jax.experimental import pallas as pl
from jax.experimental.pallas import tpu as pltpu
from jax.sharding import PartitionSpec as P


SWEEPS = 3
WIDE, NARROW = ("z_lo", "x"), ("y", "z_hi", "core")
BOTH = WIDE + NARROW
CHIPS = WIDE + NARROW[:2]
F32 = jnp.float32
BF16 = jnp.bfloat16
WHOLE = pl.BlockSpec(memory_space=pltpu.VMEM)
SCALARS = pl.BlockSpec(memory_space=pltpu.SMEM)
PX, PY = 16, 128
COLS, FREQ, NW, KW = 256, 4, 8, 512
STRIP = 24


def params(mib):
    return pltpu.CompilerParams(vmem_limit_bytes=mib << 20)


def choose_body(column_freq, data, out):
    own = data.shape[2]
    narrow = (lax.axis_index("y") * 2 + lax.axis_index("z_hi")) * 2 + lax.axis_index("core")
    shape = (own, 2 * data.shape[3])
    column = lax.broadcasted_iota(jnp.int32, shape, 0)
    freq = jnp.zeros(shape, jnp.int32)
    for j in range(own):
        freq = jnp.where(column == j, column_freq[narrow * own + j], freq)
    block = jnp.zeros(shape, F32)
    for f in range(FREQ):
        both = jnp.concatenate([data[f, 0], data[f, 1]], axis=1).astype(F32)
        block = jnp.where(freq == f, both, block)
    out[...] = jnp.broadcast_to(block.astype(BF16)[None], out.shape)


def choose(column_freq, data, receivers):
    return pl.pallas_call(
        choose_body,
        in_specs=[SCALARS, WHOLE],
        out_specs=pl.BlockSpec(),
        out_shape=jax.ShapeDtypeStruct((receivers, data.shape[2], 2 * data.shape[3]), BF16),
        compiler_params=params(8),
    )(column_freq, data)


def strip_lane(rows):
    left = (rows >= 3) & (rows < 12)
    right = (rows >= 12) & (rows < 21)
    return jnp.where(left, rows - 3, jnp.where(right, rows + (PY - 21), -1))


def adjoint_body(inv, gathered, freq, stored, classes, ops, field, strips, y_a, y_b, x_a, x_b, buf, sems, probes, masks):
    group = pl.program_id(0)
    per = buf.shape[3]

    def fetch(which, slot):
        def one(j, _):
            sensor = inv[which * per + j]
            pltpu.make_async_copy(stored.at[sensor], buf.at[slot, :, :, j], sems.at[slot]).start()
            return 0

        lax.fori_loop(0, per, one, 0, unroll=8)

    @pl.when(group == 0)
    def _():
        fetch(0, 0)
        field[...] = jnp.zeros_like(field)
        for f in range(FREQ):
            masks[f] = jnp.broadcast_to((freq[...] == f).astype(F32), (COLS, 128)).astype(BF16)

    @pl.when(group + 1 < pl.num_programs(0))
    def _():
        fetch(group + 1, (group + 1) % 2)

    slot = group % 2
    block = gathered[group]
    for f in range(FREQ):
        probes[:, f * 128 : f * 128 + 128] = block * masks[f]
    pltpu.make_async_copy(buf.at[slot], buf.at[slot], sems.at[slot]).wait()
    laid = jnp.swapaxes(buf[slot].reshape(KW, PX, PY), 0, 1)
    ops[:, pl.ds(pl.multiple_of(group * KW, KW), KW), :] = laid
    for x in range(0, PX, 2):
        pair = jnp.concatenate([laid[x], laid[x + 1]], axis=1)
        both = jnp.dot(probes[...], pair, preferred_element_type=F32)
        field[x] += both[:, :PY]
        field[x + 1] += both[:, PY:]

    @pl.when(group == pl.num_programs(0) - 1)
    def _():
        line = lax.broadcasted_iota(jnp.int32, (STRIP, 2 * PY), 0)
        lanes = lax.broadcasted_iota(jnp.int32, (STRIP, 2 * PY), 1)
        pick = (strip_lane(line) == lanes % PY).astype(F32).astype(BF16)
        nt = (((1,), (1,)), ((), ()))
        for x in range(PX):
            mine = field[x]
            high = mine.astype(BF16)
            low = (mine - high.astype(F32)).astype(BF16)
            strip = lax.dot_general(pick, jnp.concatenate([high, low], axis=1), nt, preferred_element_type=F32)
            row = jnp.broadcast_to(classes[x : x + 1, :], (PY, PY)).astype(BF16)
            label = lax.dot_general(pick[:, :PY], row, nt, preferred_element_type=F32)
            parts = (strip[:, :128], strip[:, 128:], label)
            for t in range(3):
                strips[x, t] = parts[t]
            pad = jnp.zeros((7, 128), F32)
            up = jnp.concatenate([p[18:21] for p in parts] + [pad], axis=0).astype(BF16)
            down = jnp.concatenate([p[3:6] for p in parts] + [pad], axis=0).astype(BF16)
            even = lax.axis_index(NARROW[-1]) == 0
            y_a[x] = jnp.where(even, up, down)
            y_b[x] = jnp.where(even, down, up)
        even = lax.axis_index(WIDE[-1]) % 2 == 0
        for first, out in ((jnp.where(even, PX - 3, 0), x_a), (jnp.where(even, 0, PX - 3), x_b)):
            for j in range(3):
                out[j, :COLS] = field[first + j].astype(BF16)
                row = classes[pl.ds(first + j, 1), :]
                out[j, COLS : COLS + 16] = jnp.broadcast_to(row, (16, PY)).astype(BF16)


def adjoint(inv, gathered, freq, stored, classes):
    sens = stored.shape[0]
    per = sens // NW
    y_edge = jax.ShapeDtypeStruct((PX, 16, 128), BF16)
    x_edge = jax.ShapeDtypeStruct((3, COLS + 16, PY), BF16)
    return pl.pallas_call(
        adjoint_body,
        grid=(NW,),
        in_specs=[SCALARS, WHOLE, WHOLE, pl.BlockSpec(memory_space=pltpu.HBM), WHOLE],
        out_specs=(WHOLE,) * 7,
        out_shape=(
            jax.ShapeDtypeStruct((PX, sens * FREQ * 2, PY), BF16),
            jax.ShapeDtypeStruct((PX, COLS, PY), F32),
            jax.ShapeDtypeStruct((PX, 3, STRIP, 128), F32),
            y_edge,
            y_edge,
            x_edge,
            x_edge,
        ),
        scratch_shapes=[
            pltpu.VMEM((2, FREQ, 2, per, PX, PY), BF16),
            pltpu.SemaphoreType.DMA((2,)),
            pltpu.VMEM((COLS, KW), BF16),
            pltpu.VMEM((FREQ, COLS, 128), BF16),
        ],
        compiler_params=params(24),
    )(inv, gathered, freq, stored, classes)


SROWS = 80


def halves(even, first, second):
    return jnp.where(even, second, first), jnp.where(even, first, second)


def edges_body(strips, y_a, y_b, whole, s_a, s_b):
    even = lax.axis_index(NARROW[-1]) == 0
    for x in range(PX):
        low, high = halves(even, y_a[x].astype(F32), y_b[x].astype(F32))
        for t in range(3):
            at = slice(3 * t, 3 * t + 3)
            whole[x, t] = jnp.concatenate([low[at], strips[x, t, 3:21, :], high[at]], axis=0)
    even = lax.axis_index(WIDE[-1]) % 2 == 0
    pad = jnp.zeros((SROWS - 3 * STRIP, 128), F32)
    for first, out in ((jnp.where(even, PX - 3, 0), s_a), (jnp.where(even, 0, PX - 3), s_b)):
        for j in range(3):
            out[j] = jnp.concatenate([whole[first + j, t] for t in range(3)] + [pad], axis=0).astype(BF16)


def edges(strips, y_a, y_b):
    send = jax.ShapeDtypeStruct((3, SROWS, 128), BF16)
    return pl.pallas_call(
        edges_body,
        in_specs=[WHOLE] * 3,
        out_specs=(WHOLE,) * 3,
        out_shape=(jax.ShapeDtypeStruct((PX, 3, STRIP, 128), F32), send, send),
        compiler_params=params(8),
    )(strips, y_a, y_b)


def table_of(labels, table):
    kappa = jnp.zeros(labels.shape, F32)
    for j in range(8):
        kappa = jnp.where(labels == float(j + 1), table[j], kappa)
    return kappa


def weights(here, up, down, left, right):
    four = [jnp.minimum(here, n) for n in (up, down, left, right)]
    return [1.0 - (four[0] + four[1] + four[2] + four[3])] + four


def smooth(value, load, axis, size):
    for turn in range(SWEEPS):
        fresh = []
        for i in range(1, len(value) - 1):
            m = load(i + turn)
            mid = value[i]
            left = pltpu.roll(mid, 1, axis)
            right = pltpu.roll(mid, size - 1, axis)
            a = m[0] * mid + m[1] * value[i - 1]
            b = m[2] * value[i + 1] + m[3] * left
            fresh.append(a + (b + m[4] * right))
        value = fresh
    return value


def coefficients(kappa, axis, size, out):
    for i in range(1, PX + 5):
        k = kappa[i]
        ws = weights(k, kappa[i - 1], kappa[i + 1], pltpu.roll(k, 1, axis), pltpu.roll(k, size - 1, axis))
        for d in range(5):
            out[i, d] = ws[d]


def inner_body(table, field, x_a, x_b, classes, inner, coef):
    even = lax.axis_index(WIDE[-1]) % 2 == 0

    def halo(j, rows):
        return halves(even, x_a[j, rows, :].astype(F32), x_b[j, rows, :].astype(F32))

    label = [halo(j, slice(COLS, COLS + 8)) for j in range(3)]
    own = [jnp.broadcast_to(classes[x : x + 1, :], (8, PY)) for x in range(PX)]
    label = [v[0] for v in label] + own + [v[1] for v in label]
    coefficients([table_of(v, table) for v in label], 1, PY, coef)

    def columns(g, _):
        rows = pl.ds(pl.multiple_of(g * 16, 16), 16)
        ends = [halo(j, rows) for j in range(3)]
        value = [v[0] for v in ends] + [field[x, rows, :] for x in range(PX)] + [v[1] for v in ends]

        def load(i):
            return [jnp.concatenate([coef[i, d]] * 2, axis=0) for d in range(5)]

        value = smooth(value, load, 1, PY)
        for x in range(PX):
            inner[x, rows, :] = value[x].astype(BF16)
        return 0

    lax.fori_loop(0, COLS // 16, columns, 0)


def inner_sweeps(table, field, x_a, x_b, classes):
    return pl.pallas_call(
        inner_body,
        in_specs=[SCALARS] + [WHOLE] * 4,
        out_specs=WHOLE,
        out_shape=jax.ShapeDtypeStruct((PX, COLS, PY), BF16),
        scratch_shapes=[pltpu.VMEM((PX + 6, 5, 8, PY), F32)],
        compiler_params=params(12),
    )(table, field, x_a, x_b, classes)


def outer_body(table, whole, s_a, s_b, inner, prior, coef):
    even = lax.axis_index(WIDE[-1]) % 2 == 0

    def strip_rows(t):
        rows = slice(t * STRIP, (t + 1) * STRIP)
        ends = [halves(even, s_a[j, rows, :].astype(F32), s_b[j, rows, :].astype(F32)) for j in range(3)]
        return [v[0] for v in ends] + [whole[x, t] for x in range(PX)] + [v[1] for v in ends]

    coefficients([table_of(v, table) for v in strip_rows(2)], 0, STRIP, coef)
    edge = [smooth(strip_rows(t), lambda i: [coef[i, d] for d in range(5)], 0, STRIP) for t in range(2)]
    rows = lax.broadcasted_iota(jnp.int32, (STRIP, PY), 0)
    lanes = lax.broadcasted_iota(jnp.int32, (STRIP, PY), 1)
    pick = (strip_lane(rows) == lanes).astype(F32).astype(BF16)
    lane = lax.broadcasted_iota(jnp.int32, (COLS, PY), 1)
    middle = (lane >= 3) & (lane < PY - 3)
    tn = (((0,), (0,)), ((), ()))
    for x in range(PX):
        both = jnp.concatenate([edge[0][x], edge[1][x]], axis=1).astype(BF16)
        at_edge = lax.dot_general(both, pick, tn, preferred_element_type=F32)
        prior[x] = jnp.where(middle, inner[x].astype(F32), at_edge).astype(BF16)


def outer_sweeps(table, whole, s_a, s_b, inner):
    return pl.pallas_call(
        outer_body,
        in_specs=[SCALARS] + [WHOLE] * 4,
        out_specs=WHOLE,
        out_shape=jax.ShapeDtypeStruct((PX, COLS, PY), BF16),
        scratch_shapes=[pltpu.VMEM((PX + 6, 5, STRIP, PY), F32)],
        compiler_params=params(12),
    )(table, whole, s_a, s_b, inner)


def forward_body(prior, ops, keep, send, prior_out):
    group = pl.program_id(0)
    core = lax.axis_index("core")
    rows = pl.ds(pl.multiple_of(group * KW, KW), KW)
    left = jnp.concatenate([prior[x] for x in range(PX)], axis=1)
    right = jnp.concatenate([ops[x, rows, :] for x in range(PX)], axis=1)
    nt = (((1,), (1,)), ((), ()))
    total = lax.dot_general(left, right, nt, preferred_element_type=F32)
    own = prior_out.shape[0]
    columns = pl.ds(pl.multiple_of(group * own, own), own)
    prior_out[...] = jnp.swapaxes(prior[:, columns, :], 0, 1)
    for chip in range(8):
        even = total[chip * 32 : chip * 32 + 16]
        odd = total[chip * 32 + 16 : chip * 32 + 32]
        keep[group * 8 + chip] = jnp.where(core == 0, even, odd)
        send[group * 8 + chip] = jnp.where(core == 0, odd, even).astype(BF16)


def forward(prior, ops):
    return pl.pallas_call(
        forward_body,
        grid=(NW,),
        in_specs=[WHOLE, WHOLE],
        out_specs=(WHOLE, WHOLE, pl.BlockSpec((COLS // NW, PX, PY), lambda i: (i, 0, 0))),
        out_shape=(
            jax.ShapeDtypeStruct((64, 16, KW), F32),
            jax.ShapeDtypeStruct((64, 16, KW), BF16),
            jax.ShapeDtypeStruct((COLS, PX, PY), BF16),
        ),
        compiler_params=params(16),
    )(prior, ops)


def total_body(pieces, out, *, weight):
    total = pieces[0].astype(F32)
    for chip in range(1, pieces.shape[0]):
        total = total + pieces[chip].astype(F32)
    total = (total * weight).astype(BF16)
    rows = out.shape[3]
    for f in range(FREQ):
        for q in range(2):
            at = (f * 2 + q) * rows
            out[f, q] = total[:, at : at + rows]


def reduced(keep, send, weight):
    got = lax.ppermute(send, "core", [(0, 1), (1, 0)])
    chip = (keep + got.astype(F32)).astype(BF16)
    pieces = lax.all_to_all(chip, CHIPS, 0, 0, tiled=True)
    return pl.pallas_call(
        functools.partial(total_body, weight=weight),
        in_specs=[WHOLE],
        out_specs=pl.BlockSpec(),
        out_shape=jax.ShapeDtypeStruct((FREQ, 2, pieces.shape[1], KW // (FREQ * 2)), BF16),
        compiler_params=params(8),
    )(pieces)


def swapped(first, second, axis):
    size = lax.axis_size(axis)
    odd = [(i, i + 1) for i in range(1, size - 1, 2)]
    far = lax.ppermute(second, axis, odd + [(j, i) for i, j in odd])
    near = lax.ppermute(first, axis, [(i, i ^ 1) for i in range(size)])
    return near, far


def on_device(seafloor_ops, sensor_data, column_freq, row_owner, coef_class, coef_table):
    sens = seafloor_ops.shape[0]
    per = sensor_data.shape[0]
    quad_weight = 2.0 * sens / (PX * lax.axis_size(WIDE) * PY * lax.axis_size(NARROW))
    sent = choose(column_freq, sensor_data.transpose(1, 2, 3, 0), lax.axis_size(BOTH))
    gathered = lax.all_to_all(sent, BOTH, 0, 0, tiled=True).reshape(NW, COLS, per * 2)

    ids = jnp.arange(sens, dtype=jnp.int32)
    inverse = jnp.sum(jnp.where(row_owner[None, :] == ids[:, None], ids[None, :], 0), axis=1)
    classes = (coef_class + 1).astype(F32)

    ops, field, strips, y_a, y_b, x_a, x_b = adjoint(
        inverse, gathered, column_freq.reshape(COLS, 1), seafloor_ops, classes
    )
    y_a, y_b = swapped(y_a, y_b, NARROW)
    x_a, x_b = swapped(x_a, x_b, WIDE)
    whole, s_a, s_b = edges(strips, y_a, y_b)
    s_a, s_b = swapped(s_a, s_b, WIDE)
    inner = inner_sweeps(coef_table, field, x_a, x_b, classes)
    prior = outer_sweeps(coef_table, whole, s_a, s_b, inner)
    keep, send, prior_field = forward(prior, ops)
    hessian = reduced(keep, send, quad_weight).transpose(3, 0, 1, 2)
    return hessian, prior_field


def solution(mesh):
    fine = jax.sharding.Mesh(mesh.devices.reshape(2, 4, 4, 2, 2), BOTH)
    placed = (
        P(None, None, None, WIDE, NARROW),
        P(WIDE, None, None, NARROW),
        P(),
        P(),
        P(WIDE, NARROW),
        P(),
    )
    return jax.shard_map(
        on_device,
        mesh=fine,
        in_specs=placed,
        out_specs=(P(WIDE, None, None, NARROW), P(None, WIDE, NARROW)),
        check_vma=False,
    )
```
